32 devices in a mesh: row: 4 (over y, x), col: 8 (over z, core).
Axes of the slice: x: 2, y: 2, z: 4, core: 2. Of those that a mesh axis runs over, the one named last changes fastest.
Arguments:
- block_tiles: bfloat16 [960, 512, 128], P('row', 'col'), may hold values from -1.5 to 1.5
- block_cols: int32 [960, 16], P('row', 'col'), may hold values from 0 to 119, as said below
- block_counts: int32 [960, 8], P('row', 'col'), may hold values from 0 to 2, as said below
Outputs:
- next_iterate: bfloat16 [48, 512, 128], P('row', 'col')
The draws below stay inside these ranges and needn't reach their ends.
Inputs may be any that keep to these rules, and one draw needn't show every extreme that they name: `block_cols`: within one block row and one column group, the first block_counts slots name different block columns. `block_counts`: slots at or past the count are unused.
All inputs are finite; a program needn't handle non-finite values.
Results may differ from the reference program's by a relative error of at most 0.0036.
Values may be sent and summed in bfloat16 or wider, within the bound.
No kernel may reach another device: no remote copies, remote signals or barrier semaphores. Data moves between devices by JAX's collectives and lax.ppermute only.
A program may use at most 192 MiB of HBM per device.

```python
import jax
import jax.numpy as jnp
from jax import lax

BLOCK = 64
NBLK = 960
SLOTS = 2
SLAB_ROWS = 12
N_ROW = 4
N_COL = 8


def draw_block_cols(key, part):
    width = NBLK // N_COL
    scores = jax.random.randint(key, (NBLK, N_COL, width), 0, 1 << 20) * width + jnp.arange(width, dtype=jnp.int32)
    order = jnp.argsort(scores, axis=-1)[..., :SLOTS]
    return order.reshape(NBLK, N_COL * SLOTS).astype(jnp.int32)


def draw_block_counts(key, part):
    width = NBLK // N_COL
    base = jax.random.randint(key, (NBLK, N_COL), 0, SLOTS + 1)
    row_group = jnp.arange(NBLK, dtype=jnp.int32)[:, None] // width
    near = (row_group == jnp.arange(N_COL, dtype=jnp.int32)[None, :]).astype(jnp.int32)
    counts = jnp.minimum(base + near, SLOTS).reshape(-1)
    chosen = jax.random.randint(jax.random.fold_in(key, 7), (), 0, NBLK * N_COL)
    counts = counts.at[(chosen + 1) % (NBLK * N_COL)].set(0)
    counts = counts.at[chosen].set(SLOTS)
    return counts.reshape(NBLK, N_COL).astype(jnp.int32)


def block_levels(stream_key, dims, cuts, least, high):
    loudness, own = 1.0, jax.random.fold_in(stream_key, 6)
    for position, blocks in cuts:
        heights = jnp.exp(jax.random.uniform(jax.random.fold_in(own, position), (blocks,), jnp.float32, least / len(cuts), high / len(cuts)))
        loudness = loudness * jnp.repeat(heights, dims[position] // blocks).reshape([-1 if axis == position else 1 for axis in range(len(dims))])
    return loudness


def gaussian(own_key, dims, scale, limit, shards=(), held_as=jnp.bfloat16):
    values = jax.random.normal(own_key, dims, jnp.float32) * scale
    if len(shards) > 0:
        values = block_levels(own_key, dims, shards, -0.22, 0.18) * values
    return jnp.clip(values, min=-limit, max=limit).astype(held_as)


def setup_inputs(seed: int = 0) -> dict:
    streams_of = jax.random.split(jax.random.key(seed), 4)
    return {
        "block_tiles": gaussian(streams_of[0], (NBLK, N_COL * BLOCK, SLOTS * BLOCK), 0.25, 1.5, ((0, 4), (1, 8))),
        "block_cols": draw_block_cols(jax.random.fold_in(streams_of[3], 71), 0),
        "block_counts": draw_block_counts(jax.random.fold_in(streams_of[3], 71), 0),
    }


def restricted_product(left_tiles, left_cols, left_valid, tiles, cols, valid, width):
    def one_row(operands):
        row_tiles, row_cols, row_valid = operands
        inner = (jnp.arange(N_COL, dtype=jnp.int32)[:, None] * width + row_cols).reshape(-1).astype(jnp.int32)
        fetched = tiles[inner].astype(jnp.float32)
        fetched_cols = cols[inner]
        fetched_valid = valid[inner]
        matched = (fetched_cols[:, :, None, :] == row_cols[None, :, :, None])
        matched = matched & fetched_valid[:, :, None, :] & row_valid[None, :, :, None]
        matched = matched & row_valid.reshape(-1)[:, None, None, None]
        chosen = jnp.einsum('agvw,agywz->agyvz', matched.astype(jnp.float32), fetched)
        chosen = chosen.reshape(N_COL, SLOTS, N_COL, BLOCK, SLOTS, BLOCK)
        return jnp.einsum('pxuy,pugyvz->gxvz', row_tiles, chosen)
    return lax.map(one_row, (left_tiles, left_cols, left_valid))


def reference(block_tiles, block_cols, block_counts):
    width = NBLK // N_COL
    tiles = block_tiles.reshape(NBLK, N_COL, BLOCK, SLOTS, BLOCK)
    cols = block_cols.reshape(NBLK, N_COL, SLOTS)
    valid = jnp.arange(SLOTS, dtype=jnp.int32)[None, None, :] < block_counts[:, :, None]
    slab_index = (jnp.arange(N_ROW, dtype=jnp.int32)[:, None] * (NBLK // N_ROW) + jnp.arange(SLAB_ROWS, dtype=jnp.int32)[None, :]).reshape(-1).astype(jnp.int32)
    slab_tiles = tiles[slab_index].astype(jnp.float32)
    slab_cols = cols[slab_index]
    slab_valid = valid[slab_index]
    squared = restricted_product(slab_tiles, slab_cols, slab_valid, tiles, cols, valid, width).astype(jnp.bfloat16)
    cubed = restricted_product(squared.astype(jnp.float32), slab_cols, slab_valid, tiles, cols, valid, width)
    keep = slab_valid[:, :, None, :, None]
    result = jnp.where(keep, 1.5 * slab_tiles - 0.5 * cubed, jnp.float32(0.0)).astype(jnp.bfloat16)
    return result.reshape(N_ROW * SLAB_ROWS, N_COL * BLOCK, SLOTS * BLOCK)
```

```python
import functools

import jax
import jax.numpy as jnp
from jax import lax
from jax.experimental import pallas as pl
from jax.experimental.pallas import tpu as pltpu
from jax.sharding import PartitionSpec as P

NBLK = 960
SLAB_ROWS = 12
LANES = 128
NONE = 1 << 30
LOCAL = 1 << 20


def for_sending(x):
    return jax.tree.map(lambda a: a.astype(jnp.bfloat16) if a.dtype == jnp.float32 else a, x)


def passed_along(x, axis, by):
    length = lax.axis_size(axis)
    return lax.ppermute(x, axis, [(i, (i + by) % length) for i in range(length)])


def tile_products(running, visitor, first_group, panel, own_cols, own_valid, width):
    left_tiles, left_cols, left_counts = visitor
    panel_tiles, panel_cols, panel_counts = panel
    row_count = left_cols.shape[0]
    group_count = left_cols.shape[1]
    slot_count = left_cols.shape[2]
    block_size = left_tiles.shape[2]
    offset = first_group * width
    group_tiles = lax.dynamic_slice_in_dim(panel_tiles, offset, group_count * width, 0)
    group_tiles = group_tiles.reshape(group_count, width, block_size, slot_count, block_size)
    group_cols = lax.dynamic_slice_in_dim(panel_cols, offset, group_count * width, 0).reshape(
        group_count, width, slot_count
    )
    group_counts = lax.dynamic_slice_in_dim(panel_counts, offset, group_count * width, 0).reshape(
        group_count, width
    )
    group_valid = jnp.arange(slot_count, dtype=jnp.int32)[None, None, :] < group_counts[:, :, None]
    left_valid = jnp.arange(slot_count, dtype=jnp.int32)[None, None, :] < left_counts[:, :, None]
    onehot = left_cols[:, :, :, None] == jnp.arange(width, dtype=jnp.int32)[None, None, None, :]
    matched = group_cols[None, :, None, :, :, None] == own_cols[:, None, None, None, None, :]
    matched = (
        matched & group_valid[None, :, None, :, :, None] & own_valid[:, None, None, None, None, :]
    )
    matched = matched & onehot[:, :, :, :, None, None] & left_valid[:, :, :, None, None, None]
    chosen = jnp.einsum(
        "igukwv,gkywz->iguyvz",
        matched.astype(jnp.bfloat16),
        group_tiles,
        preferred_element_type=jnp.float32,
    ).astype(jnp.bfloat16)
    left_blocks = left_tiles.reshape(row_count, group_count, block_size, slot_count, block_size)
    return running + jnp.einsum(
        "igxuy,iguyvz->ixvz", left_blocks, chosen, preferred_element_type=jnp.float32
    )


def restricted_product(left_parts, panel, own_cols, own_valid):
    col_total = lax.axis_size("col")
    row_total = lax.axis_size("row")
    width = NBLK // col_total
    slab_count = own_cols.shape[0]
    slot_count = own_cols.shape[1]
    block_size = panel[0].shape[1]
    initial = jnp.zeros((slab_count, block_size, slot_count, block_size), jnp.float32)
    ratio = col_total // row_total
    row_index = lax.axis_index("row")
    col_index = lax.axis_index("col")
    moving = left_parts
    for bit_number in range(row_total.bit_length() - 1):
        arrived = jax.tree.map(
            lambda part, own: part.astype(own.dtype),
            passed_along(for_sending(moving), "col", -(ratio << bit_number)),
            moving,
        )
        flagged = row_index // (1 << bit_number) % 2 == 1

        def select_one(incoming, current):
            return jnp.where(flagged, incoming, current)

        moving = jax.tree.map(select_one, arrived, moving)
    anchor = col_index + ratio * row_index

    def advance(section_index, carried):
        running, visiting = carried
        running = tile_products(
            running,
            visiting,
            (anchor + section_index) % col_total,
            panel,
            own_cols,
            own_valid,
            width,
        )
        visiting = jax.tree.map(
            lambda part, own: part.astype(own.dtype),
            passed_along(for_sending(visiting), "col", -1),
            visiting,
        )
        return (running, visiting)

    running, moving = lax.fori_loop(0, col_total - 1, advance, (initial, moving))
    return tile_products(
        running, moving, (anchor + col_total - 1) % col_total, panel, own_cols, own_valid, width
    )


def over_rows(x):
    row_total = lax.axis_size("row")
    return lax.all_to_all(jnp.broadcast_to(x, (row_total,) + x.shape), "row", 0, 0, tiled=True)


def dense_body(block_tiles, block_cols, block_counts):
    block_size = block_tiles.shape[1]
    slot_count = block_cols.shape[1]
    panel = (
        over_rows(block_tiles).reshape((NBLK,) + block_tiles.shape[1:]),
        over_rows(block_cols).reshape(NBLK, slot_count),
        over_rows(block_counts).reshape(NBLK),
    )
    slab_tiles = block_tiles[:SLAB_ROWS]
    own_cols = block_cols[:SLAB_ROWS]
    own_counts = block_counts[:SLAB_ROWS]
    own_valid = jnp.arange(slot_count, dtype=jnp.int32)[None, :] < own_counts
    first_parts = (
        slab_tiles.reshape(SLAB_ROWS, 1, block_size, slot_count * block_size),
        own_cols.reshape(SLAB_ROWS, 1, slot_count),
        own_counts,
    )
    squared = restricted_product(first_parts, panel, own_cols, own_valid)
    squared = squared.reshape(SLAB_ROWS, 1, block_size, slot_count * block_size).astype(
        jnp.bfloat16
    )
    second_parts = (squared, own_cols.reshape(SLAB_ROWS, 1, slot_count), own_counts)
    cubed = restricted_product(second_parts, panel, own_cols, own_valid)
    current = slab_tiles.reshape(SLAB_ROWS, block_size, slot_count, block_size).astype(jnp.float32)
    result = jnp.where(own_valid[:, None, :, None], 1.5 * current - 0.5 * cubed, jnp.float32(0.0))
    return result.reshape(SLAB_ROWS, block_size, slot_count * block_size).astype(jnp.bfloat16)


def lanes_of(x, index):
    return jnp.take_along_axis(x, index, axis=1)


def shr(x, n):
    return lax.shift_right_logical(x, jnp.broadcast_to(jnp.int32(n), x.shape) if jnp.ndim(n) == 0 else n)


def shl(x, n):
    return lax.shift_left(x, jnp.broadcast_to(jnp.int32(n), x.shape) if jnp.ndim(n) == 0 else n)


SEVENS = 0x77777777
EIGHTS = -(1 << 31) | 0x08888888


def capped_sum(x, y):
    total = x + y
    high = total & jnp.int32(EIGHTS)
    return (total & jnp.int32(SEVENS)) | (high - shr(high, 3)) & jnp.int32(SEVENS)


def plan_kernel(rows, width, meta_ref, need_ref, list_ref, view_ref, part_ref, edge_ref, state_ref, count_ref):
    r0 = lax.axis_index("row")
    c0 = lax.axis_index("col")
    lane = lax.broadcasted_iota(jnp.int32, (8, LANES), 1)
    sub = lax.broadcasted_iota(jnp.int32, (8, LANES), 0)
    slot = lane & 15
    base = lane - slot
    for r in range(4):
        for c in range(8):
            piece = meta_ref[r * 8 + c]
            for h in range(2):
                part_ref[2 * r + h, 2 * c : 2 * c + 2, :] = piece[:, h * LANES : (h + 1) * LANES]
    lane16 = lax.broadcasted_iota(jnp.int32, (16, LANES), 1)
    sub16 = lax.broadcasted_iota(jnp.int32, (16, LANES), 0)
    diagonal = sub16 == (lane16 & 15)
    bit16 = shl(jnp.ones_like(sub16), sub16)
    low16 = (sub16 & 1) == 0
    parts = [part_ref[j] for j in range(8)]

    def gather16(x, index):
        return jnp.concatenate([lanes_of(x[:8], index[:8]), lanes_of(x[8:], index[8:])], 0)

    for r in range(4):
        for half in range(2):
            i16 = (lane16 >> 4) + 8 * half
            own = gather16(parts[2 * r], i16)
            own = jnp.where(i16 < rows, own, -1)
            col = jnp.sum(jnp.where(diagonal, own, 0), axis=0, keepdims=True)
            lane1 = lax.broadcasted_iota(jnp.int32, (1, LANES), 1)
            k = ((lane1 & 15) >> 1) * width + col
            there = (col >= 0).astype(jnp.int32)
            rk = (k >= 240).astype(jnp.int32) + (k >= 480).astype(jnp.int32) + (k >= 720).astype(jnp.int32)
            n = k - 240 * rk
            where_k = jnp.where(there > 0, 2 * rk + (n >> 7), -1)
            at = jnp.broadcast_to(n & (LANES - 1), (16, LANES))
            piece_k = jnp.broadcast_to(where_k, (16, LANES))
            found = jnp.full((16, LANES), -2, jnp.int32)
            for j in range(8):
                found = jnp.where(piece_k == j, gather16(parts[j], at), found)
            up = jnp.concatenate([pltpu.roll(found[:8], 7, 0), pltpu.roll(found[8:], 7, 0)], 0)
            down = jnp.concatenate([pltpu.roll(found[:8], 1, 0), pltpu.roll(found[8:], 1, 0)], 0)
            other = jnp.where(low16, up, down)
            same = (found == own) & (own >= 0)
            cross = (other == own) & (own >= 0)
            out = jnp.sum(jnp.where(same | cross, bit16, 0), axis=0, keepdims=True)
            low_slot = (same & low16) | (cross & ~low16)
            high_slot = (same | cross) & ~low_slot
            which = jnp.sum(jnp.where(high_slot, bit16, 0), axis=0, keepdims=True)
            s = 2 * r + half
            state_ref[0, s : s + 1, :] = out
            state_ref[1, s : s + 1, :] = which
            state_ref[2, s : s + 1, :] = jnp.where(there > 0, k, -1)
    out = state_ref[0]
    which = state_ref[1]
    k = state_ref[2]
    rk = (k >= 240).astype(jnp.int32) + (k >= 480).astype(jnp.int32) + (k >= 720).astype(jnp.int32)
    rsub = sub >> 1
    row = (sub & 1) * 8 + (lane >> 4)

    into = jnp.zeros_like(out)
    for a in range(16):
        into = into | shl(shr(lanes_of(out, base + a), slot) & 1, a)
    spread = (out | shr(out, 1)) & 0x5555
    spread = (spread | shl(spread, 8)) & 0x00FF00FF
    spread = (spread | shl(spread, 4)) & 0x0F0F0F0F
    spread = (spread | shl(spread, 2)) & 0x11111111
    on_diag = (k == rsub * 240 + row) & (k >= 0)
    diag = jnp.where(on_diag, slot, -1)
    for step in (1, 2, 4, 8):
        diag = jnp.maximum(diag, lanes_of(diag, lane ^ step))
    has_diag = diag >= 0
    diag_at = base + jnp.maximum(diag, 0)
    left = jnp.zeros_like(out)
    extra = jnp.zeros_like(out)
    edges = []
    for b in range(16):
        has = (shr(out, b) & 1) > 0
        heads = lanes_of(spread, base + b)
        left = left | jnp.where(has, heads, 0)
        edge = jnp.where(has, heads | jnp.where(into != 0, 1 << (4 * (b // 2)), 0), 0)
        extra = extra | jnp.where((slot == b) & has_diag, lanes_of(edge, diag_at), 0)
        edges.append(jnp.where(on_diag, 0, edge))
    left = left | extra

    fifteen = jnp.full_like(out, 15)
    sent_left = left & ~shl(fifteen, 4 * (slot >> 1))
    sent = []
    bits = jnp.where((shr(left, 4 * c0) & 1) > 0, 1 << 16, 0)
    for b in range(16):
        own_nibble = (15 << (4 * (b // 2))) if b < 14 else -(1 << 28)
        sent.append(edges[b] & ~jnp.where(rk == rsub, jnp.int32(own_nibble), 0))
        edge_ref[b] = sent[b]
        bits = bits | jnp.where((shr(edges[b], 4 * c0) & 1) > 0, 1 << b, 0)

    words = []
    for p in range(8):
        for r in range(4):
            word = capped_sum(jnp.where(rk == r, sent[2 * p], 0), jnp.where(rk == r, sent[2 * p + 1], 0))
            word = capped_sum(word, jnp.where((rsub == r) & ((slot >> 1) == p), sent_left, 0))
            words.append(word)
    span = LANES // 2
    while len(words) > 1:
        merged = []
        first = (lane & span) == 0
        for x, y in zip(words[0::2], words[1::2]):
            xx = capped_sum(x, pltpu.roll(x, LANES - span, 1))
            yy = capped_sum(y, pltpu.roll(y, span, 1))
            merged.append(jnp.where(first, xx, yy))
        words = merged
        span //= 2
    word = words[0]
    while span >= 1:
        word = capped_sum(word, lanes_of(word, lane ^ span))
        span //= 2
    word = capped_sum(word, pltpu.roll(word, 7, 0))
    most = jnp.zeros_like(word)
    for g in range(8):
        most = jnp.maximum(most, shr(word, 4 * g) & 15)
    most = jnp.where((sub & 1) == 0, most, 0)
    needed = jnp.max(most)
    need_ref[0] = needed

    mine = rsub == r0
    view_ref[0] = jnp.where(mine, bits, 0)
    view_ref[1] = jnp.where(mine & (into != 0), shr(out, 2 * c0) & 3, 0)
    view_ref[2] = into
    view_ref[3] = which
    view_ref[4] = k
    view_ref[5] = diag

    from_left = jnp.where(mine & ((slot >> 1) == c0), sent_left, 0)
    from_rows = [jnp.where(rk == r0, edge_ref[2 * c0 + v], 0) for v in range(2)]
    masks = [from_left] + from_rows
    place = sub * LANES + lane
    busy = jnp.where((masks[0] | masks[1] | masks[2]) != 0, place, NONE)
    state_ref[3] = busy
    for d in range(32):
        count_ref[d] = 0
    local = k - 240 * r0

    def pick(x, hit):
        return jnp.sum(jnp.where(hit, x, 0))

    def send_from(carried):
        spot, total = carried
        hit = place == spot
        r = lax.shift_right_logical(spot, 8)
        picked_which = pick(which, hit)
        picked_row = pick(local, hit)
        slab_row = (lax.shift_right_logical(spot, 7) & 1) * 8 + (lax.shift_right_logical(spot, 4) & 7)
        sources = [
            2 * slab_row + (spot & 1),
            2 * picked_row + (lax.shift_right_logical(picked_which, 2 * c0) & 1),
            2 * picked_row + (lax.shift_right_logical(picked_which, 2 * c0 + 1) & 1),
        ]
        for source, mask in zip(sources, masks):
            nibbles = pick(mask, hit)

            def to_group(g, total):
                on = lax.shift_right_logical(nibbles, 4 * g) & 1

                @pl.when(on > 0)
                def _():
                    d = r * 8 + g
                    list_ref[1 + 2 * total] = count_ref[d] * 32 + d
                    list_ref[2 + 2 * total] = source
                    count_ref[d] = count_ref[d] + 1

                return total + on

            total = lax.cond(nibbles != 0, lambda t: lax.fori_loop(0, 8, to_group, t), lambda t: t, total)
        left_over = jnp.where(hit, NONE, state_ref[3])
        state_ref[3] = left_over
        return jnp.min(left_over), total

    first_spot = jnp.where(needed <= 4, jnp.min(busy), NONE)
    _, total = lax.while_loop(lambda s: s[0] < NONE, send_from, (first_spot, jnp.int32(0)))
    list_ref[0] = total


def pack_kernel(cap, list_ref, tiles_ref, out_ref, held_ref, sem):
    total = list_ref[0]

    def fetch(t):
        return pltpu.make_async_copy(tiles_ref.at[list_ref[2 + 2 * t] >> 1], held_ref.at[t], sem)

    @pl.loop(0, total)
    def _(t):
        fetch(t).start()

    @pl.loop(0, total)
    def _(t):
        fetch(t).wait()

    @pl.loop(0, total)
    def _(t):
        to = list_ref[1 + 2 * t]
        high = list_ref[2 + 2 * t] & 1
        tile = held_ref[t].astype(jnp.float32)
        tile = jnp.where(high > 0, pltpu.roll(tile, 64, 1), tile)
        upper = lax.broadcasted_iota(jnp.int32, (32, LANES), 1) >= 64
        chunk = jnp.where(upper, pltpu.roll(tile[32:], 64, 1), tile[:32])
        out_ref[to & 31, to >> 5] = chunk.astype(jnp.bfloat16)


def apply_kernel(cap, view_ref, got_ref, tiles_ref, slab_ref, count_col_ref, out_ref, extra_ref, place_ref, state_ref, count_ref, held_ref, sem):
    r0 = lax.axis_index("row")
    c0 = lax.axis_index("col")
    me = r0 * 8 + c0
    lane = lax.broadcasted_iota(jnp.int32, (8, LANES), 1)
    sub = lax.broadcasted_iota(jnp.int32, (8, LANES), 0)
    place = sub * LANES + lane
    bits = view_ref[0]
    k = view_ref[4]
    which = view_ref[3]
    for d in range(32):
        count_ref[d] = 0

    def pick(x, hit):
        return jnp.sum(jnp.where(hit, x, 0))

    state_ref[0] = jnp.where(bits != 0, place, NONE)

    def arrive(spot):
        hit = place == spot
        at = spot - 256 * r0
        picked = pick(bits, hit)
        picked_k = pick(k, hit)
        picked_which = pick(which, hit)
        source_row = picked_k // 240

        def put(entry, source, held_at):
            @pl.when(source == me)
            def _():
                place_ref[entry] = LOCAL + held_at

            @pl.when(source != me)
            def _():
                place_ref[entry] = source * cap + count_ref[source]
                count_ref[source] = count_ref[source] + 1

        @pl.when((picked >> 16) > 0)
        def _():
            put(4096 + at, r0 * 8 + ((at & 15) >> 1), 2 * (at >> 4) + (at & 1))

        @pl.loop(0, 16)
        def _(b):
            @pl.when(((picked >> b) & 1) > 0)
            def _():
                put(
                    at * 16 + b,
                    source_row * 8 + (b >> 1),
                    2 * (picked_k - 240 * source_row) + ((picked_which >> b) & 1),
                )

        left_over = jnp.where(hit, NONE, state_ref[0])
        state_ref[0] = left_over
        return jnp.min(left_over)

    lax.while_loop(lambda s: s < NONE, arrive, jnp.min(state_ref[0]))

    def tile_at(entry):
        where = place_ref[entry]

        @pl.when(where >= LOCAL)
        def _():
            copy = pltpu.make_async_copy(tiles_ref.at[(where - LOCAL) >> 1], held_ref, sem)
            copy.start()
            copy.wait()
            tile = held_ref[...].astype(jnp.float32)
            state_tile = jnp.where((where & 1) > 0, pltpu.roll(tile, 64, 1), tile)
            extra_ref[13] = state_tile

        @pl.when(where < LOCAL)
        def _():
            chunk = got_ref[where // cap, where % cap].astype(jnp.float32)
            extra_ref[13, :32, :] = chunk
            extra_ref[13, 32:, :] = pltpu.roll(chunk, 64, 1)

        return extra_ref[13][:, :64].astype(jnp.bfloat16)

    extra_ref[:SLAB_ROWS] = jnp.zeros((SLAB_ROWS, 64, LANES), jnp.float32)
    heads = view_ref[1]
    into = view_ref[2]
    diag = view_ref[5]
    state_ref[1] = jnp.where(heads != 0, place, NONE)

    def follow(spot):
        hit = place == spot
        at = spot - 256 * r0
        i = at >> 4
        b = at & 15
        tails = pick(into, hit)
        ends = pick(heads, hit)
        self_slot = pick(diag, hit)
        extra_ref[12] = jnp.zeros((64, LANES), jnp.float32)

        @pl.loop(0, 16)
        def _(a):
            @pl.when(((tails >> a) & 1) > 0)
            def _():
                x = tile_at(4096 + i * 16 + a)
                y = tile_at(jnp.where(a == self_slot, 4096 + i * 16 + b, (i * 16 + a) * 16 + b))
                extra_ref[12, :, :64] += jnp.dot(x, y, preferred_element_type=jnp.float32)

        squared = extra_ref[12][:, :64].astype(jnp.bfloat16)
        for v in range(2):

            @pl.when(((ends >> v) & 1) > 0)
            def _():
                c = 2 * c0 + v
                y = tile_at(jnp.where(b == self_slot, 4096 + i * 16 + c, at * 16 + c))
                extra_ref[i, :, 64 * v : 64 * v + 64] += jnp.dot(squared, y, preferred_element_type=jnp.float32)

        left_over = jnp.where(hit, NONE, state_ref[1])
        state_ref[1] = left_over
        return jnp.min(left_over)

    lax.while_loop(lambda s: s < NONE, follow, jnp.min(state_ref[1]))

    high = (lax.broadcasted_iota(jnp.int32, (64, LANES), 1) >= 64).astype(jnp.int32)
    for i in range(SLAB_ROWS):
        keep = high < count_col_ref[i]
        x = slab_ref[i].astype(jnp.float32)
        out_ref[i] = jnp.where(keep, 1.5 * x - 0.5 * extra_ref[i], 0.0).astype(jnp.bfloat16)


def sparse_body(block_tiles, block_cols, block_counts):
    row_total = lax.axis_size("row")
    col_total = lax.axis_size("col")
    devices = row_total * col_total
    per_device = block_cols.shape[0]
    slots = jnp.arange(2, dtype=jnp.int32)[None, :]
    shown = jnp.where(slots < block_counts, block_cols, -1).T
    shown = jnp.pad(shown, ((0, 0), (0, 256 - per_device)), constant_values=-1)
    meta = lax.all_to_all(
        jnp.broadcast_to(shown, (devices, 2, 256)), ("row", "col"), 0, 0, tiled=True
    )
    vmem = pl.BlockSpec(memory_space=pltpu.VMEM)
    smem = pl.BlockSpec(memory_space=pltpu.SMEM)
    anywhere = pl.BlockSpec(memory_space=pl.ANY)
    need, sends, view = pl.pallas_call(
        functools.partial(plan_kernel, SLAB_ROWS, NBLK // col_total),
        name="plan",
        in_specs=[vmem],
        out_specs=(smem, smem, vmem),
        out_shape=(
            jax.ShapeDtypeStruct((1,), jnp.int32),
            jax.ShapeDtypeStruct((256,), jnp.int32),
            jax.ShapeDtypeStruct((6, 8, LANES), jnp.int32),
        ),
        scratch_shapes=[
            pltpu.VMEM((8, 16, LANES), jnp.int32),
            pltpu.VMEM((16, 8, LANES), jnp.int32),
            pltpu.VMEM((4, 8, LANES), jnp.int32),
            pltpu.SMEM((32,), jnp.int32),
        ],
    )(meta)
    slab_counts = block_counts[:SLAB_ROWS, 0]
    slab = block_tiles[:SLAB_ROWS]

    def exchanged(cap):
        def run():
            packed = pl.pallas_call(
                functools.partial(pack_kernel, cap),
                name="pack",
                in_specs=[smem, anywhere],
                out_specs=vmem,
                out_shape=jax.ShapeDtypeStruct((devices, cap, 32, LANES), jnp.bfloat16),
                scratch_shapes=[pltpu.VMEM((124, 64, LANES), jnp.bfloat16), pltpu.SemaphoreType.DMA],
            )(sends, block_tiles)
            got = lax.all_to_all(packed, ("row", "col"), 0, 0, tiled=True)
            return pl.pallas_call(
                functools.partial(apply_kernel, cap),
                name="apply",
                in_specs=[vmem, vmem, anywhere, vmem, smem],
                out_specs=vmem,
                out_shape=jax.ShapeDtypeStruct((SLAB_ROWS, 64, LANES), jnp.bfloat16),
                scratch_shapes=[
                    pltpu.VMEM((14, 64, LANES), jnp.float32),
                    pltpu.SMEM((4096 + 256,), jnp.int32),
                    pltpu.VMEM((2, 8, LANES), jnp.int32),
                    pltpu.SMEM((32,), jnp.int32),
                    pltpu.VMEM((64, LANES), jnp.bfloat16),
                    pltpu.SemaphoreType.DMA,
                ],
            )(view, got, block_tiles, slab, slab_counts)

        return run

    rounds = need[0]
    branch = jnp.where(rounds <= 1, 0, jnp.where(rounds <= 2, 1, jnp.where(rounds <= 4, 2, 3)))
    return lax.switch(
        branch,
        [
            exchanged(1),
            exchanged(2),
            exchanged(4),
            lambda: dense_body(block_tiles, block_cols, block_counts),
        ],
    )


def solution(mesh):
    small = dict(mesh.shape) == {"row": 4, "col": 8}
    return jax.shard_map(
        sparse_body if small else dense_body,
        mesh=mesh,
        in_specs=(P("row", "col", None), P("row", "col"), P("row", "col")),
        out_specs=P("row", "col", None),
        check_vma=False,
    )
```

```python
import functools

import jax
import jax.numpy as jnp
from jax import lax
from jax.experimental import pallas as pl
from jax.experimental.pallas import tpu as pltpu
from jax.sharding import PartitionSpec as P

NBLK = 960
SLAB_ROWS = 12
LANES = 128
NONE = 1 << 30
LOCAL = 1 << 20
VMEM_LIMIT = 24 << 20


def for_sending(x):
    return jax.tree.map(lambda a: a.astype(jnp.bfloat16) if a.dtype == jnp.float32 else a, x)


def passed_along(x, axis, by):
    length = lax.axis_size(axis)
    return lax.ppermute(x, axis, [(i, (i + by) % length) for i in range(length)])


def tile_products(running, visitor, first_group, panel, own_cols, own_valid, width):
    left_tiles, left_cols, left_counts = visitor
    panel_tiles, panel_cols, panel_counts = panel
    row_count = left_cols.shape[0]
    group_count = left_cols.shape[1]
    slot_count = left_cols.shape[2]
    block_size = left_tiles.shape[2]
    offset = first_group * width
    group_tiles = lax.dynamic_slice_in_dim(panel_tiles, offset, group_count * width, 0)
    group_tiles = group_tiles.reshape(group_count, width, block_size, slot_count, block_size)
    group_cols = lax.dynamic_slice_in_dim(panel_cols, offset, group_count * width, 0).reshape(
        group_count, width, slot_count
    )
    group_counts = lax.dynamic_slice_in_dim(panel_counts, offset, group_count * width, 0).reshape(
        group_count, width
    )
    group_valid = jnp.arange(slot_count, dtype=jnp.int32)[None, None, :] < group_counts[:, :, None]
    left_valid = jnp.arange(slot_count, dtype=jnp.int32)[None, None, :] < left_counts[:, :, None]
    onehot = left_cols[:, :, :, None] == jnp.arange(width, dtype=jnp.int32)[None, None, None, :]
    matched = group_cols[None, :, None, :, :, None] == own_cols[:, None, None, None, None, :]
    matched = (
        matched & group_valid[None, :, None, :, :, None] & own_valid[:, None, None, None, None, :]
    )
    matched = matched & onehot[:, :, :, :, None, None] & left_valid[:, :, :, None, None, None]
    chosen = jnp.einsum(
        "igukwv,gkywz->iguyvz",
        matched.astype(jnp.bfloat16),
        group_tiles,
        preferred_element_type=jnp.float32,
    ).astype(jnp.bfloat16)
    left_blocks = left_tiles.reshape(row_count, group_count, block_size, slot_count, block_size)
    return running + jnp.einsum(
        "igxuy,iguyvz->ixvz", left_blocks, chosen, preferred_element_type=jnp.float32
    )


def restricted_product(left_parts, panel, own_cols, own_valid):
    col_total = lax.axis_size("col")
    row_total = lax.axis_size("row")
    width = NBLK // col_total
    slab_count = own_cols.shape[0]
    slot_count = own_cols.shape[1]
    block_size = panel[0].shape[1]
    initial = jnp.zeros((slab_count, block_size, slot_count, block_size), jnp.float32)
    ratio = col_total // row_total
    row_index = lax.axis_index("row")
    col_index = lax.axis_index("col")
    moving = left_parts
    for bit_number in range(row_total.bit_length() - 1):
        arrived = jax.tree.map(
            lambda part, own: part.astype(own.dtype),
            passed_along(for_sending(moving), "col", -(ratio << bit_number)),
            moving,
        )
        flagged = row_index // (1 << bit_number) % 2 == 1

        def select_one(incoming, current):
            return jnp.where(flagged, incoming, current)

        moving = jax.tree.map(select_one, arrived, moving)
    anchor = col_index + ratio * row_index

    def advance(section_index, carried):
        running, visiting = carried
        running = tile_products(
            running,
            visiting,
            (anchor + section_index) % col_total,
            panel,
            own_cols,
            own_valid,
            width,
        )
        visiting = jax.tree.map(
            lambda part, own: part.astype(own.dtype),
            passed_along(for_sending(visiting), "col", -1),
            visiting,
        )
        return (running, visiting)

    running, moving = lax.fori_loop(0, col_total - 1, advance, (initial, moving))
    return tile_products(
        running, moving, (anchor + col_total - 1) % col_total, panel, own_cols, own_valid, width
    )


def over_rows(x):
    row_total = lax.axis_size("row")
    return lax.all_to_all(jnp.broadcast_to(x, (row_total,) + x.shape), "row", 0, 0, tiled=True)


def dense_body(block_tiles, block_cols, block_counts):
    block_size = block_tiles.shape[1]
    slot_count = block_cols.shape[1]
    panel = (
        over_rows(block_tiles).reshape((NBLK,) + block_tiles.shape[1:]),
        over_rows(block_cols).reshape(NBLK, slot_count),
        over_rows(block_counts).reshape(NBLK),
    )
    slab_tiles = block_tiles[:SLAB_ROWS]
    own_cols = block_cols[:SLAB_ROWS]
    own_counts = block_counts[:SLAB_ROWS]
    own_valid = jnp.arange(slot_count, dtype=jnp.int32)[None, :] < own_counts
    first_parts = (
        slab_tiles.reshape(SLAB_ROWS, 1, block_size, slot_count * block_size),
        own_cols.reshape(SLAB_ROWS, 1, slot_count),
        own_counts,
    )
    squared = restricted_product(first_parts, panel, own_cols, own_valid)
    squared = squared.reshape(SLAB_ROWS, 1, block_size, slot_count * block_size).astype(
        jnp.bfloat16
    )
    second_parts = (squared, own_cols.reshape(SLAB_ROWS, 1, slot_count), own_counts)
    cubed = restricted_product(second_parts, panel, own_cols, own_valid)
    current = slab_tiles.reshape(SLAB_ROWS, block_size, slot_count, block_size).astype(jnp.float32)
    result = jnp.where(own_valid[:, None, :, None], 1.5 * current - 0.5 * cubed, jnp.float32(0.0))
    return result.reshape(SLAB_ROWS, block_size, slot_count * block_size).astype(jnp.bfloat16)


def lanes_of(x, index):
    return jnp.take_along_axis(x, index, axis=1)


def shr(x, n):
    return lax.shift_right_logical(x, jnp.broadcast_to(jnp.int32(n), x.shape) if jnp.ndim(n) == 0 else n)


def shl(x, n):
    return lax.shift_left(x, jnp.broadcast_to(jnp.int32(n), x.shape) if jnp.ndim(n) == 0 else n)


SEVENS = 0x77777777
EIGHTS = -(1 << 31) | 0x08888888


def capped_sum(x, y):
    total = x + y
    high = total & jnp.int32(EIGHTS)
    return (total & jnp.int32(SEVENS)) | (high - shr(high, 3)) & jnp.int32(SEVENS)


def packed_tile(tile, high):
    tile = tile.astype(jnp.float32)
    tile = jnp.where(high > 0, pltpu.roll(tile, 64, 1), tile)
    upper = lax.broadcasted_iota(jnp.int32, (32, LANES), 1) >= 64
    return jnp.where(upper, pltpu.roll(tile[32:], 64, 1), tile[:32]).astype(jnp.bfloat16)


def plan_kernel(
    rows, width, meta_ref, tiles_ref, need_ref, list_ref, view_ref, first_ref, second_ref, part_ref, edge_ref, state_ref, count_ref, held_ref, sem
):
    fetch = pltpu.make_async_copy(tiles_ref, held_ref, sem)
    fetch.start()
    r0 = lax.axis_index("row")
    c0 = lax.axis_index("col")
    lane = lax.broadcasted_iota(jnp.int32, (8, LANES), 1)
    sub = lax.broadcasted_iota(jnp.int32, (8, LANES), 0)
    slot = lane & 15
    base = lane - slot
    for r in range(4):
        for c in range(8):
            piece = meta_ref[r * 8 + c]
            part_ref[2 * r, 2 * c : 2 * c + 2, :] = piece[:, :LANES]
            part_ref[2 * r + 1, 2 * c : 2 * c + 2, : piece.shape[1] - LANES] = piece[:, LANES:]
    lane16 = lax.broadcasted_iota(jnp.int32, (16, LANES), 1)
    sub16 = lax.broadcasted_iota(jnp.int32, (16, LANES), 0)
    diagonal = sub16 == (lane16 & 15)
    bit16 = shl(jnp.ones_like(sub16), sub16)
    low16 = (sub16 & 1) == 0
    parts = [part_ref[j] for j in range(8)]

    def gather16(x, index):
        return jnp.concatenate([lanes_of(x[:8], index[:8]), lanes_of(x[8:], index[8:])], 0)

    for r in range(4):
        for half in range(2):
            i16 = (lane16 >> 4) + 8 * half
            own = gather16(parts[2 * r], i16)
            own = jnp.where(i16 < rows, own, -1)
            col = jnp.sum(jnp.where(diagonal, own, 0), axis=0, keepdims=True)
            lane1 = lax.broadcasted_iota(jnp.int32, (1, LANES), 1)
            k = ((lane1 & 15) >> 1) * width + col
            there = (col >= 0).astype(jnp.int32)
            rk = (k >= 240).astype(jnp.int32) + (k >= 480).astype(jnp.int32) + (k >= 720).astype(jnp.int32)
            n = k - 240 * rk
            where_k = jnp.where(there > 0, 2 * rk + (n >> 7), -1)
            at = jnp.broadcast_to(n & (LANES - 1), (16, LANES))
            piece_k = jnp.broadcast_to(where_k, (16, LANES))
            found = jnp.full((16, LANES), -2, jnp.int32)
            for j in range(8):
                found = jnp.where(piece_k == j, gather16(parts[j], at), found)
            up = jnp.concatenate([pltpu.roll(found[:8], 7, 0), pltpu.roll(found[8:], 7, 0)], 0)
            down = jnp.concatenate([pltpu.roll(found[:8], 1, 0), pltpu.roll(found[8:], 1, 0)], 0)
            other = jnp.where(low16, up, down)
            same = (found == own) & (own >= 0)
            cross = (other == own) & (own >= 0)
            out = jnp.sum(jnp.where(same | cross, bit16, 0), axis=0, keepdims=True)
            low_slot = (same & low16) | (cross & ~low16)
            high_slot = (same | cross) & ~low_slot
            which = jnp.sum(jnp.where(high_slot, bit16, 0), axis=0, keepdims=True)
            s = 2 * r + half
            state_ref[0, s : s + 1, :] = out
            state_ref[1, s : s + 1, :] = which
            state_ref[2, s : s + 1, :] = jnp.where(there > 0, k, -1)
    out = state_ref[0]
    which = state_ref[1]
    k = state_ref[2]
    rk = (k >= 240).astype(jnp.int32) + (k >= 480).astype(jnp.int32) + (k >= 720).astype(jnp.int32)
    rsub = sub >> 1
    row = (sub & 1) * 8 + (lane >> 4)

    into = jnp.zeros_like(out)
    for a in range(16):
        into = into | shl(shr(lanes_of(out, base + a), slot) & 1, a)
    spread = (out | shr(out, 1)) & 0x5555
    spread = (spread | shl(spread, 8)) & 0x00FF00FF
    spread = (spread | shl(spread, 4)) & 0x0F0F0F0F
    spread = (spread | shl(spread, 2)) & 0x11111111
    on_diag = (k == rsub * 240 + row) & (k >= 0)
    diag = jnp.where(on_diag, slot, -1)
    for step in (1, 2, 4, 8):
        diag = jnp.maximum(diag, lanes_of(diag, lane ^ step))
    has_diag = diag >= 0
    diag_at = base + jnp.maximum(diag, 0)
    left = jnp.zeros_like(out)
    extra = jnp.zeros_like(out)
    edges = []
    for b in range(16):
        has = (shr(out, b) & 1) > 0
        heads = lanes_of(spread, base + b)
        left = left | jnp.where(has, heads, 0)
        edge = jnp.where(has, heads | jnp.where(into != 0, 1 << (4 * (b // 2)), 0), 0)
        extra = extra | jnp.where((slot == b) & has_diag, lanes_of(edge, diag_at), 0)
        edges.append(jnp.where(on_diag, 0, edge))
    left = left | extra

    fifteen = jnp.full_like(out, 15)
    sent_left = left & ~shl(fifteen, 4 * (slot >> 1))
    sent = []
    bits = jnp.where((shr(left, 4 * c0) & 1) > 0, 1 << 16, 0)
    for b in range(16):
        own_nibble = (15 << (4 * (b // 2))) if b < 14 else -(1 << 28)
        sent.append(edges[b] & ~jnp.where(rk == rsub, jnp.int32(own_nibble), 0))
        edge_ref[b] = sent[b]
        bits = bits | jnp.where((shr(edges[b], 4 * c0) & 1) > 0, 1 << b, 0)

    words = []
    for p in range(8):
        for r in range(4):
            word = capped_sum(jnp.where(rk == r, sent[2 * p], 0), jnp.where(rk == r, sent[2 * p + 1], 0))
            word = capped_sum(word, jnp.where((rsub == r) & ((slot >> 1) == p), sent_left, 0))
            words.append(word)
    span = LANES // 2
    while len(words) > 1:
        merged = []
        first = (lane & span) == 0
        for x, y in zip(words[0::2], words[1::2]):
            xx = capped_sum(x, pltpu.roll(x, LANES - span, 1))
            yy = capped_sum(y, pltpu.roll(y, span, 1))
            merged.append(jnp.where(first, xx, yy))
        words = merged
        span //= 2
    word = words[0]
    while span >= 1:
        word = capped_sum(word, lanes_of(word, lane ^ span))
        span //= 2
    word = capped_sum(word, pltpu.roll(word, 7, 0))
    most = jnp.zeros_like(word)
    for g in range(8):
        most = jnp.maximum(most, shr(word, 4 * g) & 15)
    most = jnp.where((sub & 1) == 0, most, 0)
    needed = jnp.max(most)
    need_ref[0] = jnp.where(needed <= 1, 0, jnp.where(needed <= 2, 1, jnp.where(needed <= 4, 2, 3)))

    mine = rsub == r0
    view_ref[0] = jnp.where(mine, bits, 0)
    view_ref[1] = jnp.where(mine & (into != 0), shr(out, 2 * c0) & 3, 0)
    view_ref[2] = into
    view_ref[3] = which
    view_ref[4] = k
    view_ref[5] = diag

    from_left = jnp.where(mine & ((slot >> 1) == c0), sent_left, 0)
    from_rows = [jnp.where(rk == r0, edge_ref[2 * c0 + v], 0) for v in range(2)]
    masks = [from_left] + from_rows
    place = sub * LANES + lane
    busy = jnp.where((masks[0] | masks[1] | masks[2]) != 0, place, NONE)
    state_ref[3] = busy
    for d in range(32):
        count_ref[d] = 0
    local = k - 240 * r0

    def pick(x, hit):
        return jnp.sum(jnp.where(hit, x, 0))

    def send_from(carried):
        spot, total = carried
        hit = place == spot
        r = lax.shift_right_logical(spot, 8)
        picked_which = pick(which, hit)
        picked_row = pick(local, hit)
        slab_row = (lax.shift_right_logical(spot, 7) & 1) * 8 + (lax.shift_right_logical(spot, 4) & 7)
        sources = [
            2 * slab_row + (spot & 1),
            2 * picked_row + (lax.shift_right_logical(picked_which, 2 * c0) & 1),
            2 * picked_row + (lax.shift_right_logical(picked_which, 2 * c0 + 1) & 1),
        ]
        for source, mask in zip(sources, masks):
            nibbles = pick(mask, hit)

            def to_groups(total):
                chunk = packed_tile(held_ref[source >> 1], source & 1)

                def to_group(g, total):
                    on = lax.shift_right_logical(nibbles, 4 * g) & 1

                    @pl.when(on > 0)
                    def _():
                        d = r * 8 + g
                        seen = count_ref[d]
                        list_ref[1 + 2 * total] = seen * 32 + d
                        list_ref[2 + 2 * total] = source
                        count_ref[d] = seen + 1

                        @pl.when(seen == 0)
                        def _():
                            first_ref[d, 0] = chunk

                        @pl.when(seen == 1)
                        def _():
                            second_ref[d, 0] = chunk

                    return total + on

                return lax.fori_loop(0, 8, to_group, total)

            total = lax.cond(nibbles != 0, to_groups, lambda t: t, total)
        left_over = jnp.where(hit, NONE, state_ref[3])
        state_ref[3] = left_over
        return jnp.min(left_over), total

    fetch.wait()
    first_spot = jnp.where(needed <= 4, jnp.min(busy), NONE)
    _, total = lax.while_loop(lambda s: s[0] < NONE, send_from, (first_spot, jnp.int32(0)))
    list_ref[0] = total


def pack_kernel(list_ref, tiles_ref, out_ref):
    @pl.loop(0, list_ref[0])
    def _(t):
        to = list_ref[1 + 2 * t]
        source = list_ref[2 + 2 * t]
        out_ref[to & 31, to >> 5] = packed_tile(tiles_ref[source >> 1], source & 1)


def apply_kernel(cap, view_ref, got_ref, tiles_ref, slab_count_ref, out_ref, extra_ref, place_ref, state_ref, count_ref):
    r0 = lax.axis_index("row")
    c0 = lax.axis_index("col")
    me = r0 * 8 + c0
    lane = lax.broadcasted_iota(jnp.int32, (8, LANES), 1)
    sub = lax.broadcasted_iota(jnp.int32, (8, LANES), 0)
    place = sub * LANES + lane
    bits = view_ref[0]
    k = view_ref[4]
    which = view_ref[3]
    for d in range(32):
        count_ref[d] = 0

    def pick(x, hit):
        return jnp.sum(jnp.where(hit, x, 0))

    state_ref[0] = jnp.where(bits != 0, place, NONE)

    def arrive(spot):
        hit = place == spot
        at = spot - 256 * r0
        picked = pick(bits, hit)
        picked_k = pick(k, hit)
        picked_which = pick(which, hit)
        source_row = picked_k // 240

        def put(entry, source, held_at):
            @pl.when(source == me)
            def _():
                place_ref[entry] = LOCAL + held_at

            @pl.when(source != me)
            def _():
                place_ref[entry] = source * cap + count_ref[source]
                count_ref[source] = count_ref[source] + 1

        @pl.when((picked >> 16) > 0)
        def _():
            put(4096 + at, r0 * 8 + ((at & 15) >> 1), 2 * (at >> 4) + (at & 1))

        @pl.loop(0, 16)
        def _(b):
            @pl.when(((picked >> b) & 1) > 0)
            def _():
                put(
                    at * 16 + b,
                    source_row * 8 + (b >> 1),
                    2 * (picked_k - 240 * source_row) + ((picked_which >> b) & 1),
                )

        left_over = jnp.where(hit, NONE, state_ref[0])
        state_ref[0] = left_over
        return jnp.min(left_over)

    lax.while_loop(lambda s: s < NONE, arrive, jnp.min(state_ref[0]))

    def tile_at(entry):
        where = place_ref[entry]

        @pl.when(where >= LOCAL)
        def _():
            tile = tiles_ref[(where - LOCAL) >> 1].astype(jnp.float32)
            extra_ref[13] = jnp.where((where & 1) > 0, pltpu.roll(tile, 64, 1), tile)

        @pl.when(where < LOCAL)
        def _():
            chunk = got_ref[where // cap, where % cap].astype(jnp.float32)
            extra_ref[13, :32, :] = chunk
            extra_ref[13, 32:, :] = pltpu.roll(chunk, 64, 1)

        return extra_ref[13][:, :64].astype(jnp.bfloat16)

    extra_ref[:SLAB_ROWS] = jnp.zeros((SLAB_ROWS, 64, LANES), jnp.float32)
    heads = view_ref[1]
    into = view_ref[2]
    diag = view_ref[5]
    state_ref[1] = jnp.where(heads != 0, place, NONE)

    def follow(spot):
        hit = place == spot
        at = spot - 256 * r0
        i = at >> 4
        b = at & 15
        tails = pick(into, hit)
        ends = pick(heads, hit)
        self_slot = pick(diag, hit)
        extra_ref[12] = jnp.zeros((64, LANES), jnp.float32)

        @pl.loop(0, 16)
        def _(a):
            @pl.when(((tails >> a) & 1) > 0)
            def _():
                x = tile_at(4096 + i * 16 + a)
                y = tile_at(jnp.where(a == self_slot, 4096 + i * 16 + b, (i * 16 + a) * 16 + b))
                extra_ref[12, :, :64] += jnp.dot(x, y, preferred_element_type=jnp.float32)

        squared = extra_ref[12][:, :64].astype(jnp.bfloat16)
        for v in range(2):

            @pl.when(((ends >> v) & 1) > 0)
            def _():
                c = 2 * c0 + v
                y = tile_at(jnp.where(b == self_slot, 4096 + i * 16 + c, at * 16 + c))
                extra_ref[i, :, 64 * v : 64 * v + 64] += jnp.dot(squared, y, preferred_element_type=jnp.float32)

        left_over = jnp.where(hit, NONE, state_ref[1])
        state_ref[1] = left_over
        return jnp.min(left_over)

    lax.while_loop(lambda s: s < NONE, follow, jnp.min(state_ref[1]))

    high = (lax.broadcasted_iota(jnp.int32, (64, LANES), 1) >= 64).astype(jnp.int32)
    for i in range(SLAB_ROWS):
        keep = high < slab_count_ref[i]
        x = tiles_ref[i].astype(jnp.float32)
        out_ref[i] = jnp.where(keep, 1.5 * x - 0.5 * extra_ref[i], 0.0).astype(jnp.bfloat16)


def sparse_body(block_tiles, block_cols, block_counts):
    row_total = lax.axis_size("row")
    col_total = lax.axis_size("col")
    devices = row_total * col_total
    per_device = block_cols.shape[0]
    slots = jnp.arange(2, dtype=jnp.int32)[:, None]
    shown = jnp.where(slots < block_counts.T, block_cols.T, -1)
    meta = lax.all_to_all(
        jnp.broadcast_to(shown, (devices, 2, per_device)), ("row", "col"), 0, 0, tiled=True
    )
    vmem = pl.BlockSpec(memory_space=pltpu.VMEM)
    smem = pl.BlockSpec(memory_space=pltpu.SMEM)
    anywhere = pl.BlockSpec(memory_space=pl.ANY)
    limit = pltpu.CompilerParams(vmem_limit_bytes=VMEM_LIMIT)
    chunk = jax.ShapeDtypeStruct((devices, 1, 32, LANES), jnp.bfloat16)
    branch, sends, view, first, second = pl.pallas_call(
        functools.partial(plan_kernel, SLAB_ROWS, NBLK // col_total),
        name="plan",
        in_specs=[vmem, anywhere],
        out_specs=(smem, smem, vmem, vmem, vmem),
        out_shape=(
            jax.ShapeDtypeStruct((1,), jnp.int32),
            jax.ShapeDtypeStruct((256,), jnp.int32),
            jax.ShapeDtypeStruct((6, 8, LANES), jnp.int32),
            chunk,
            chunk,
        ),
        scratch_shapes=[
            pltpu.VMEM((8, 16, LANES), jnp.int32),
            pltpu.VMEM((16, 8, LANES), jnp.int32),
            pltpu.VMEM((4, 8, LANES), jnp.int32),
            pltpu.SMEM((32,), jnp.int32),
            pltpu.VMEM(block_tiles.shape, block_tiles.dtype),
            pltpu.SemaphoreType.DMA,
        ],
        compiler_params=limit,
    )(meta, block_tiles)
    slab_counts = block_counts[:SLAB_ROWS, 0]

    def applied(cap, packed):
        got = lax.all_to_all(packed, ("row", "col"), 0, 0, tiled=True)
        return pl.pallas_call(
            functools.partial(apply_kernel, cap),
            name="apply",
            in_specs=[vmem, vmem, vmem, smem],
            out_specs=vmem,
            out_shape=jax.ShapeDtypeStruct((SLAB_ROWS, 64, LANES), jnp.bfloat16),
            scratch_shapes=[
                pltpu.VMEM((14, 64, LANES), jnp.float32),
                pltpu.SMEM((4096 + 256,), jnp.int32),
                pltpu.VMEM((2, 8, LANES), jnp.int32),
                pltpu.SMEM((32,), jnp.int32),
            ],
            compiler_params=limit,
        )(view, got, block_tiles, slab_counts)

    def four():
        packed = pl.pallas_call(
            pack_kernel,
            name="pack",
            in_specs=[smem, vmem],
            out_specs=vmem,
            out_shape=jax.ShapeDtypeStruct((devices, 4, 32, LANES), jnp.bfloat16),
            compiler_params=limit,
        )(sends, block_tiles)
        return applied(4, packed)

    return lax.switch(
        branch[0],
        [
            lambda: applied(1, first),
            lambda: applied(2, jnp.concatenate([first, second], 1)),
            four,
            lambda: dense_body(block_tiles, block_cols, block_counts),
        ],
    )


def solution(mesh):
    small = dict(mesh.shape) == {"row": 4, "col": 8}
    return jax.shard_map(
        sparse_body if small else dense_body,
        mesh=mesh,
        in_specs=(P("row", "col", None), P("row", "col"), P("row", "col")),
        out_specs=P("row", "col", None),
        check_vma=False,
    )
```

```python
import functools

import jax
import jax.numpy as jnp
from jax import lax
from jax.experimental import pallas as pl
from jax.experimental.pallas import tpu as pltpu
from jax.sharding import PartitionSpec as P

NBLK = 960
SLAB_ROWS = 12
LANES = 128
NONE = 1 << 30
LOCAL = 1 << 20
CAPS = (1, 2, 3, 4, 7)
OWN = 16
OWN_AT = 1 << 16
PREFIX = 1024
PROGRAM = 7168
VMEM_LIMIT = 24 << 20


def for_sending(x):
    return jax.tree.map(lambda a: a.astype(jnp.bfloat16) if a.dtype == jnp.float32 else a, x)


def passed_along(x, axis, by):
    length = lax.axis_size(axis)
    return lax.ppermute(x, axis, [(i, (i + by) % length) for i in range(length)])


def tile_products(running, visitor, first_group, panel, own_cols, own_valid, width):
    left_tiles, left_cols, left_counts = visitor
    panel_tiles, panel_cols, panel_counts = panel
    row_count = left_cols.shape[0]
    group_count = left_cols.shape[1]
    slot_count = left_cols.shape[2]
    block_size = left_tiles.shape[2]
    offset = first_group * width
    group_tiles = lax.dynamic_slice_in_dim(panel_tiles, offset, group_count * width, 0)
    group_tiles = group_tiles.reshape(group_count, width, block_size, slot_count, block_size)
    group_cols = lax.dynamic_slice_in_dim(panel_cols, offset, group_count * width, 0).reshape(
        group_count, width, slot_count
    )
    group_counts = lax.dynamic_slice_in_dim(panel_counts, offset, group_count * width, 0).reshape(
        group_count, width
    )
    group_valid = jnp.arange(slot_count, dtype=jnp.int32)[None, None, :] < group_counts[:, :, None]
    left_valid = jnp.arange(slot_count, dtype=jnp.int32)[None, None, :] < left_counts[:, :, None]
    onehot = left_cols[:, :, :, None] == jnp.arange(width, dtype=jnp.int32)[None, None, None, :]
    matched = group_cols[None, :, None, :, :, None] == own_cols[:, None, None, None, None, :]
    matched = (
        matched & group_valid[None, :, None, :, :, None] & own_valid[:, None, None, None, None, :]
    )
    matched = matched & onehot[:, :, :, :, None, None] & left_valid[:, :, :, None, None, None]
    chosen = jnp.einsum(
        "igukwv,gkywz->iguyvz",
        matched.astype(jnp.bfloat16),
        group_tiles,
        preferred_element_type=jnp.float32,
    ).astype(jnp.bfloat16)
    left_blocks = left_tiles.reshape(row_count, group_count, block_size, slot_count, block_size)
    return running + jnp.einsum(
        "igxuy,iguyvz->ixvz", left_blocks, chosen, preferred_element_type=jnp.float32
    )


def restricted_product(left_parts, panel, own_cols, own_valid):
    col_total = lax.axis_size("col")
    row_total = lax.axis_size("row")
    width = NBLK // col_total
    slab_count = own_cols.shape[0]
    slot_count = own_cols.shape[1]
    block_size = panel[0].shape[1]
    initial = jnp.zeros((slab_count, block_size, slot_count, block_size), jnp.float32)
    ratio = col_total // row_total
    row_index = lax.axis_index("row")
    col_index = lax.axis_index("col")
    moving = left_parts
    for bit_number in range(row_total.bit_length() - 1):
        arrived = jax.tree.map(
            lambda part, own: part.astype(own.dtype),
            passed_along(for_sending(moving), "col", -(ratio << bit_number)),
            moving,
        )
        flagged = row_index // (1 << bit_number) % 2 == 1

        def select_one(incoming, current):
            return jnp.where(flagged, incoming, current)

        moving = jax.tree.map(select_one, arrived, moving)
    anchor = col_index + ratio * row_index

    def advance(section_index, carried):
        running, visiting = carried
        running = tile_products(
            running,
            visiting,
            (anchor + section_index) % col_total,
            panel,
            own_cols,
            own_valid,
            width,
        )
        visiting = jax.tree.map(
            lambda part, own: part.astype(own.dtype),
            passed_along(for_sending(visiting), "col", -1),
            visiting,
        )
        return (running, visiting)

    running, moving = lax.fori_loop(0, col_total - 1, advance, (initial, moving))
    return tile_products(
        running, moving, (anchor + col_total - 1) % col_total, panel, own_cols, own_valid, width
    )


def over_rows(x):
    row_total = lax.axis_size("row")
    return lax.all_to_all(jnp.broadcast_to(x, (row_total,) + x.shape), "row", 0, 0, tiled=True)


def dense_body(block_tiles, block_cols, block_counts):
    block_size = block_tiles.shape[1]
    slot_count = block_cols.shape[1]
    panel = (
        over_rows(block_tiles).reshape((NBLK,) + block_tiles.shape[1:]),
        over_rows(block_cols).reshape(NBLK, slot_count),
        over_rows(block_counts).reshape(NBLK),
    )
    slab_tiles = block_tiles[:SLAB_ROWS]
    own_cols = block_cols[:SLAB_ROWS]
    own_counts = block_counts[:SLAB_ROWS]
    own_valid = jnp.arange(slot_count, dtype=jnp.int32)[None, :] < own_counts
    first_parts = (
        slab_tiles.reshape(SLAB_ROWS, 1, block_size, slot_count * block_size),
        own_cols.reshape(SLAB_ROWS, 1, slot_count),
        own_counts,
    )
    squared = restricted_product(first_parts, panel, own_cols, own_valid)
    squared = squared.reshape(SLAB_ROWS, 1, block_size, slot_count * block_size).astype(
        jnp.bfloat16
    )
    second_parts = (squared, own_cols.reshape(SLAB_ROWS, 1, slot_count), own_counts)
    cubed = restricted_product(second_parts, panel, own_cols, own_valid)
    current = slab_tiles.reshape(SLAB_ROWS, block_size, slot_count, block_size).astype(jnp.float32)
    result = jnp.where(own_valid[:, None, :, None], 1.5 * current - 0.5 * cubed, jnp.float32(0.0))
    return result.reshape(SLAB_ROWS, block_size, slot_count * block_size).astype(jnp.bfloat16)


def lanes_of(x, index):
    return jnp.take_along_axis(x, index, axis=1)


def shr(x, n):
    return lax.shift_right_logical(x, jnp.broadcast_to(jnp.int32(n), x.shape) if jnp.ndim(n) == 0 else n)


def shl(x, n):
    return lax.shift_left(x, jnp.broadcast_to(jnp.int32(n), x.shape) if jnp.ndim(n) == 0 else n)


SEVENS = 0x77777777
EIGHTS = -(1 << 31) | 0x08888888


def capped(x):
    high = x & jnp.int32(EIGHTS)
    return (x & jnp.int32(SEVENS)) | (high - shr(high, 3))


def packed_tile(tile, high):
    tile = tile.astype(jnp.float32)
    tile = jnp.where(high > 0, pltpu.roll(tile, 64, 1), tile)
    upper = lax.broadcasted_iota(jnp.int32, (32, LANES), 1) >= 64
    return jnp.where(upper, pltpu.roll(tile[32:], 64, 1), tile[:32]).astype(jnp.bfloat16)


def show_kernel(cols_ref, counts_ref, out_ref):
    cols = cols_ref[...]
    slots = lax.broadcasted_iota(jnp.int32, cols.shape, 0)
    shown = jnp.where(slots < jnp.broadcast_to(counts_ref[...], cols.shape), cols, -1)
    for d in range(out_ref.shape[0]):
        out_ref[d] = shown


def hold_kernel(tiles_ref, count_ref, held_ref, base_ref, keep_ref, sem):
    fetch = pltpu.make_async_copy(tiles_ref.at[:SLAB_ROWS], held_ref, sem)
    fetch.start()
    lane = lax.broadcasted_iota(jnp.int32, (8, LANES), 1)
    sub = lax.broadcasted_iota(jnp.int32, (8, LANES), 0)
    counts = jnp.broadcast_to(count_ref[:, :LANES], (8, LANES))
    upper = (lane >= 64).astype(jnp.int32)
    for part in range(2):
        keep_ref[8 * part : 8 * part + 8, :] = (upper < lanes_of(counts, sub + 8 * part)).astype(jnp.int32)
    fetch.wait()
    for i in range(SLAB_ROWS):
        keep = jnp.broadcast_to(keep_ref[i : i + 1, :], (64, LANES)) > 0
        base_ref[i] = jnp.where(keep, 1.5 * held_ref[i].astype(jnp.float32), 0.0).astype(jnp.bfloat16)


def plan_kernel(rows, width, meta_ref, tiles_ref, need_ref, view_ref, *rest):
    send_refs = rest[: len(CAPS)]
    (
        part_ref, edge_ref, state_ref, list_ref, count_ref, begin_ref, fetched_ref, chunk_ref, sem, out_sem
    ) = rest[len(CAPS) :]
    r0 = lax.axis_index("row")
    c0 = lax.axis_index("col")
    lane = lax.broadcasted_iota(jnp.int32, (8, LANES), 1)
    sub = lax.broadcasted_iota(jnp.int32, (8, LANES), 0)
    slot = lane & 15
    base = lane - slot
    for r in range(4):
        for c in range(8):
            piece = meta_ref[r * 8 + c]
            part_ref[2 * r, 2 * c : 2 * c + 2, :] = piece[:, :LANES]
            part_ref[2 * r + 1, 2 * c : 2 * c + 2, : piece.shape[1] - LANES] = piece[:, LANES:]
    lane16 = lax.broadcasted_iota(jnp.int32, (16, LANES), 1)
    sub16 = lax.broadcasted_iota(jnp.int32, (16, LANES), 0)
    diagonal = sub16 == (lane16 & 15)
    bit16 = shl(jnp.ones_like(sub16), sub16)
    low16 = (sub16 & 1) == 0
    parts = [part_ref[j] for j in range(8)]

    def gather16(x, index):
        return jnp.concatenate([lanes_of(x[:8], index[:8]), lanes_of(x[8:], index[8:])], 0)

    for r in range(4):
        for half in range(2):
            i16 = (lane16 >> 4) + 8 * half
            own = gather16(parts[2 * r], i16)
            own = jnp.where(i16 < rows, own, -1)
            col = jnp.sum(jnp.where(diagonal, own, 0), axis=0, keepdims=True)
            lane1 = lax.broadcasted_iota(jnp.int32, (1, LANES), 1)
            k = ((lane1 & 15) >> 1) * width + col
            there = (col >= 0).astype(jnp.int32)
            rk = (k >= 240).astype(jnp.int32) + (k >= 480).astype(jnp.int32) + (k >= 720).astype(jnp.int32)
            n = k - 240 * rk
            where_k = jnp.where(there > 0, 2 * rk + (n >> 7), -1)
            at = jnp.broadcast_to(n & (LANES - 1), (16, LANES))
            piece_k = jnp.broadcast_to(where_k, (16, LANES))
            found = jnp.full((16, LANES), -2, jnp.int32)
            for j in range(8):
                found = jnp.where(piece_k == j, gather16(parts[j], at), found)
            up = jnp.concatenate([pltpu.roll(found[:8], 7, 0), pltpu.roll(found[8:], 7, 0)], 0)
            down = jnp.concatenate([pltpu.roll(found[:8], 1, 0), pltpu.roll(found[8:], 1, 0)], 0)
            other = jnp.where(low16, up, down)
            same = (found == own) & (own >= 0)
            cross = (other == own) & (own >= 0)
            out = jnp.sum(jnp.where(same | cross, bit16, 0), axis=0, keepdims=True)
            low_slot = (same & low16) | (cross & ~low16)
            high_slot = (same | cross) & ~low_slot
            which = jnp.sum(jnp.where(high_slot, bit16, 0), axis=0, keepdims=True)
            s = 2 * r + half
            state_ref[0, s : s + 1, :] = out
            state_ref[1, s : s + 1, :] = which
            state_ref[2, s : s + 1, :] = jnp.where(there > 0, k, -1)
    out = state_ref[0]
    which = state_ref[1]
    k = state_ref[2]
    rk = (k >= 240).astype(jnp.int32) + (k >= 480).astype(jnp.int32) + (k >= 720).astype(jnp.int32)
    rsub = sub >> 1
    row = (sub & 1) * 8 + (lane >> 4)

    into = jnp.zeros_like(out)
    for a in range(16):
        into = into | shl(shr(lanes_of(out, base + a), slot) & 1, a)
    spread = (out | shr(out, 1)) & 0x5555
    spread = (spread | shl(spread, 8)) & 0x00FF00FF
    spread = (spread | shl(spread, 4)) & 0x0F0F0F0F
    spread = (spread | shl(spread, 2)) & 0x11111111
    on_diag = (k == rsub * 240 + row) & (k >= 0)
    diag = jnp.where(on_diag, slot, -1)
    for step in (1, 2, 4, 8):
        diag = jnp.maximum(diag, lanes_of(diag, lane ^ step))
    has_diag = diag >= 0
    diag_at = base + jnp.maximum(diag, 0)
    left = jnp.zeros_like(out)
    extra = jnp.zeros_like(out)
    edges = []
    for b in range(16):
        has = (shr(out, b) & 1) > 0
        heads = lanes_of(spread, base + b)
        left = left | jnp.where(has, heads, 0)
        edge = jnp.where(has, heads | jnp.where(into != 0, 1 << (4 * (b // 2)), 0), 0)
        extra = extra | jnp.where((slot == b) & has_diag, lanes_of(edge, diag_at), 0)
        edges.append(jnp.where(on_diag, 0, edge))
    left = left | extra

    fifteen = jnp.full_like(out, 15)
    sent_left = left & ~shl(fifteen, 4 * (slot >> 1))
    sent = []
    bits = jnp.where((shr(left, 4 * c0) & 1) > 0, 1 << 16, 0)
    for b in range(16):
        own_nibble = (15 << (4 * (b // 2))) if b < 14 else -(1 << 28)
        sent.append(edges[b] & ~jnp.where(rk == rsub, jnp.int32(own_nibble), 0))
        edge_ref[b] = sent[b]
        bits = bits | jnp.where((shr(edges[b], 4 * c0) & 1) > 0, 1 << b, 0)

    words = []
    for p in range(8):
        pair = sent[2 * p] + sent[2 * p + 1]
        for r in range(4):
            words.append(jnp.where(rk == r, pair, 0))
    span = LANES // 2
    while len(words) > 1:
        if len(words) == 8:
            words = [capped(x) for x in words]
        merged = []
        first = (lane & span) == 0
        for x, y in zip(words[0::2], words[1::2]):
            z = jnp.where(first, x, y) + lanes_of(jnp.where(first, y, x), lane ^ span)
            merged.append(z if len(words) > 8 else capped(z))
        words = merged
        span //= 2
    word = words[0]
    while span >= 1:
        word = capped(word + lanes_of(word, lane ^ span))
        span //= 2
    by_slot = sent_left + lanes_of(sent_left, lane ^ 1)
    by_slot = by_slot + lanes_of(by_slot, lane ^ 64)
    by_slot = capped(by_slot + lanes_of(by_slot, lane ^ 32))
    by_slot = capped(by_slot + lanes_of(by_slot, lane ^ 16))
    group = (shr(lane, 4) & 1) | (shr(lane, 2) & 2) | (lane & 4)
    from_row = (shr(lane, 6) & 1) | (shr(lane, 4) & 2)
    word = capped(word + jnp.where(from_row == rsub, lanes_of(by_slot, 2 * group), 0))
    word = capped(word + pltpu.roll(word, 7, 0))
    most = jnp.zeros_like(word)
    for g in range(8):
        most = jnp.maximum(most, shr(word, 4 * g) & 15)
    most = jnp.where((sub & 1) == 0, most, 0)
    needed = jnp.max(most)
    chosen = jnp.int32(0)
    for cap in CAPS:
        chosen = chosen + (needed > cap).astype(jnp.int32)
    need_ref[0] = chosen

    mine = rsub == r0
    view_ref[0] = jnp.where(mine, bits, 0)
    view_ref[1] = jnp.where(mine & (into != 0), shr(out, 2 * c0) & 3, 0)
    view_ref[2] = into
    view_ref[3] = which
    view_ref[4] = k
    view_ref[5] = diag

    from_left = jnp.where(mine & ((slot >> 1) == c0), sent_left, 0)
    from_rows = [jnp.where(rk == r0, edge_ref[2 * c0 + v], 0) for v in range(2)]
    masks = [from_left] + from_rows
    place = sub * LANES + lane
    busy = jnp.where((masks[0] | masks[1] | masks[2]) != 0, place, NONE)
    state_ref[3] = busy
    for d in range(32):
        count_ref[d] = 0
    local = k - 240 * r0

    def pick(x, hit):
        return jnp.sum(jnp.where(hit, x, 0))

    def send_from(carried):
        spot, fetched, total = carried
        hit = place == spot
        left_over = jnp.where(hit, NONE, state_ref[3])
        state_ref[3] = left_over
        following = jnp.min(left_over)
        r = lax.shift_right_logical(spot, 8)
        picked_which = pick(which, hit)
        picked_row = pick(local, hit)
        picked = [pick(mask, hit) for mask in masks]
        slab_row = (lax.shift_right_logical(spot, 7) & 1) * 8 + (lax.shift_right_logical(spot, 4) & 7)
        sources = [
            2 * slab_row + (spot & 1),
            2 * picked_row + (lax.shift_right_logical(picked_which, 2 * c0) & 1),
            2 * picked_row + (lax.shift_right_logical(picked_which, 2 * c0 + 1) & 1),
        ]
        for source, nibbles in zip(sources, picked):

            def to_groups(carried):
                fetched, total = carried
                pltpu.make_async_copy(tiles_ref.at[source >> 1], fetched_ref.at[fetched], sem).start()
                begin_ref[fetched] = total
                for g in range(8):
                    on = lax.shift_right_logical(nibbles, 4 * g) & 1
                    d = r * 8 + g
                    seen = count_ref[d]
                    list_ref[2 * total] = seen * 32 + d
                    list_ref[2 * total + 1] = source
                    count_ref[d] = seen + on
                    total = total + on
                return fetched + 1, total

            fetched, total = lax.cond(nibbles != 0, to_groups, lambda t: t, (fetched, total))
        return following, fetched, total

    first_spot = jnp.where(needed <= CAPS[-1], jnp.min(busy), NONE)
    _, fetched, total = lax.while_loop(
        lambda s: s[0] < NONE, send_from, (first_spot, jnp.int32(0), jnp.int32(0))
    )
    begin_ref[fetched] = total

    @pl.loop(0, fetched)
    def _(n):
        pltpu.make_async_copy(tiles_ref.at[0], fetched_ref.at[n], sem).wait()

    @pl.loop(0, fetched)
    def _(n):
        chunk_ref[n] = packed_tile(fetched_ref[n], list_ref[2 * begin_ref[n] + 1] & 1)

    for index, send_ref in enumerate(send_refs):

        @pl.when((chosen == index) & (total > 0))
        def _(send_ref=send_ref):
            @pl.loop(0, fetched)
            def _(n):
                @pl.loop(begin_ref[n], begin_ref[n + 1])
                def _(t):
                    to = list_ref[2 * t]
                    pltpu.make_async_copy(chunk_ref.at[n], send_ref.at[to & 31, to >> 5], out_sem).start()

            @pl.loop(0, total)
            def _(t):
                pltpu.make_async_copy(chunk_ref.at[0], send_ref.at[0, 0], out_sem).wait()


def route_kernel(
    cap, view_ref, tiles_ref, program_ref, own_ref, place_ref, state_ref, count_ref, kept_ref, fetched_ref, sem
):
    r0 = lax.axis_index("row")
    c0 = lax.axis_index("col")
    me = r0 * 8 + c0
    lane = lax.broadcasted_iota(jnp.int32, (8, LANES), 1)
    sub = lax.broadcasted_iota(jnp.int32, (8, LANES), 0)
    place = sub * LANES + lane
    bits = view_ref[0]
    heads = view_ref[1]
    into = view_ref[2]
    which = view_ref[3]
    k = view_ref[4]
    diag = view_ref[5]
    for d in range(32):
        count_ref[d] = 0
    kept_ref[0] = 0

    def pick(x, hit):
        return jnp.sum(jnp.where(hit, x, 0))

    state_ref[0] = jnp.where(bits != 0, place, NONE)

    def arrive(spot):
        hit = place == spot
        left_over = jnp.where(hit, NONE, state_ref[0])
        state_ref[0] = left_over
        following = jnp.min(left_over)
        at = spot - 256 * r0
        picked = pick(bits, hit)
        picked_k = pick(k, hit)
        picked_which = pick(which, hit)
        source_row = picked_k // 240

        def put(entry, source, held_at):
            @pl.when(source == me)
            def _():
                kept = kept_ref[0]
                place_ref[entry] = jnp.where(kept < OWN, OWN_AT + kept, LOCAL + held_at)

                @pl.when(kept < OWN)
                def _():
                    pltpu.make_async_copy(tiles_ref.at[held_at >> 1], fetched_ref.at[kept], sem).start()
                    kept_ref[0] = kept + 1
                    kept_ref[1 + kept] = held_at

            @pl.when(source != me)
            def _():
                place_ref[entry] = source * cap + count_ref[source]
                count_ref[source] = count_ref[source] + 1

        @pl.when((picked >> 16) > 0)
        def _():
            put(4096 + at, r0 * 8 + ((at & 15) >> 1), 2 * (at >> 4) + (at & 1))

        @pl.loop(0, 16)
        def _(b):
            @pl.when(((picked >> b) & 1) > 0)
            def _():
                put(
                    at * 16 + b,
                    source_row * 8 + (b >> 1),
                    2 * (picked_k - 240 * source_row) + ((picked_which >> b) & 1),
                )

        return following

    lax.while_loop(lambda s: s < NONE, arrive, jnp.min(state_ref[0]))
    state_ref[1] = jnp.where(heads != 0, place, NONE)

    def follow(carried):
        spot, head_count, p = carried
        hit = place == spot
        left_over = jnp.where(hit, NONE, state_ref[1])
        state_ref[1] = left_over
        following = jnp.min(left_over)
        at = spot - 256 * r0
        i = at >> 4
        b = at & 15
        tails = pick(into, hit)
        ends = pick(heads, hit)
        self_slot = pick(diag, hit)
        program_ref[p] = i
        for v in range(2):
            c = 2 * c0 + v
            entry = jnp.where(b == self_slot, 4096 + i * 16 + c, at * 16 + c)
            program_ref[p + 2 + v] = jnp.where(((ends >> v) & 1) > 0, place_ref[entry], -1)

        def tail(a, count):
            on = (tails >> a) & 1

            @pl.when(on > 0)
            def _():
                q = p + 4 + 2 * count
                program_ref[q] = place_ref[4096 + i * 16 + a]
                program_ref[q + 1] = place_ref[
                    jnp.where(a == self_slot, 4096 + i * 16 + b, (i * 16 + a) * 16 + b)
                ]

            return count + on

        count = lax.fori_loop(0, 16, tail, jnp.int32(0))
        program_ref[p + 1] = count
        return following, head_count + 1, p + 4 + 2 * count

    _, head_count, end = lax.while_loop(
        lambda s: s[0] < NONE, follow, (jnp.min(state_ref[1]), jnp.int32(0), jnp.int32(2))
    )
    program_ref[0] = head_count
    program_ref[1] = end
    kept = kept_ref[0]

    @pl.loop(0, kept)
    def _(n):
        pltpu.make_async_copy(tiles_ref.at[0], fetched_ref.at[n], sem).wait()

    @pl.loop(0, kept)
    def _(n):
        own_ref[n] = packed_tile(fetched_ref[n], kept_ref[1 + n] & 1)


def apply_kernel(
    cap,
    program_hbm,
    got_ref,
    own_ref,
    tiles_ref,
    slab_ref,
    base_ref,
    keep_ref,
    out_ref,
    program_ref,
    cube_ref,
    touched_ref,
    patch_ref,
    spare_ref,
    sem,
    patch_sem,
    spare_sem,
    program_sem,
):
    load = pltpu.make_async_copy(program_hbm.at[:PREFIX], program_ref.at[:PREFIX], program_sem)
    load.start()
    write = pltpu.make_async_copy(base_ref, out_ref, sem)
    write.start()
    for i in range(SLAB_ROWS):
        touched_ref[i] = 0
    low = lax.broadcasted_iota(jnp.int32, (32, LANES), 1) < 64
    load.wait()

    @pl.when(program_ref[1] > PREFIX)
    def _():
        rest = pltpu.make_async_copy(program_hbm, program_ref, program_sem)
        rest.start()
        rest.wait()

    def tile_at(where):
        def near():
            got_at = jnp.minimum(where, 32 * cap - 1)
            own_at = jnp.clip(where - OWN_AT, 0, OWN - 1)
            return jnp.where(where < OWN_AT, got_ref[got_at // cap, got_at % cap], own_ref[own_at])

        def far():
            copy = pltpu.make_async_copy(tiles_ref.at[(where - LOCAL) >> 1], spare_ref, spare_sem)
            copy.start()
            copy.wait()
            return packed_tile(spare_ref[...], where & 1)

        return lax.cond(where < LOCAL, near, far)

    def twice(tile):
        x = tile.astype(jnp.float32)
        y = pltpu.roll(x, 64, 1)
        zero = jnp.zeros_like(x)
        return jnp.concatenate(
            [jnp.where(low, x, zero), jnp.where(low, y, zero), jnp.where(low, zero, y), jnp.where(low, zero, x)], 0
        ).astype(jnp.bfloat16)

    def product(x, y):
        return jnp.dot(x, twice(y), preferred_element_type=jnp.float32)

    def head(_, p):
        i = program_ref[p]
        count = program_ref[p + 1]

        def tail(t, total):
            q = p + 4 + 2 * t
            return total + product(tile_at(program_ref[q]), tile_at(program_ref[q + 1]))

        total = lax.fori_loop(0, count, tail, jnp.zeros((32, LANES), jnp.float32))
        squared = total.astype(jnp.bfloat16)

        @pl.when(touched_ref[i] == 0)
        def _():
            touched_ref[i] = 1
            cube_ref[i] = jnp.zeros((2, 32, LANES), jnp.float32)

        for v in range(2):
            where = program_ref[p + 2 + v]

            @pl.when(where >= 0)
            def _():
                cube_ref[i, v] += product(squared, tile_at(where))

        return p + 4 + 2 * count

    lax.fori_loop(0, program_ref[0], head, jnp.int32(2))
    write.wait()

    def patch(i):
        return pltpu.make_async_copy(patch_ref.at[i], out_ref.at[i], patch_sem.at[i])

    @pl.loop(0, SLAB_ROWS)
    def _(i):
        @pl.when(touched_ref[i] > 0)
        def _():
            x = cube_ref[i, 0]
            y = cube_ref[i, 1]
            cubed = jnp.concatenate(
                [jnp.where(low, x, pltpu.roll(y, 64, 1)), jnp.where(low, pltpu.roll(x, 64, 1), y)], 0
            )
            keep = jnp.broadcast_to(keep_ref[pl.ds(i, 1), :], (64, LANES)) > 0
            current = slab_ref[i].astype(jnp.float32)
            patch_ref[i] = jnp.where(keep, 1.5 * current - 0.5 * cubed, 0.0).astype(jnp.bfloat16)
            patch(i).start()

    @pl.loop(0, SLAB_ROWS)
    def _(i):
        @pl.when(touched_ref[i] > 0)
        def _():
            patch(i).wait()


def sparse_body(block_tiles, block_cols, block_counts):
    row_total = lax.axis_size("row")
    col_total = lax.axis_size("col")
    devices = row_total * col_total
    per_device = block_cols.shape[0]
    shown = pl.pallas_call(
        show_kernel,
        name="show",
        out_shape=jax.ShapeDtypeStruct((devices, 2, per_device), jnp.int32),
        compiler_params=pltpu.CompilerParams(vmem_limit_bytes=VMEM_LIMIT),
    )(block_cols.T, block_counts.T)
    meta = lax.all_to_all(shown, ("row", "col"), 0, 0, tiled=True)
    vmem = pl.BlockSpec(memory_space=pltpu.VMEM)
    smem = pl.BlockSpec(memory_space=pltpu.SMEM)
    anywhere = pl.BlockSpec(memory_space=pl.ANY)
    limit = pltpu.CompilerParams(vmem_limit_bytes=VMEM_LIMIT)
    slab, base, keep = pl.pallas_call(
        hold_kernel,
        name="hold",
        in_specs=[anywhere, vmem],
        out_specs=(vmem, vmem, vmem),
        out_shape=(
            jax.ShapeDtypeStruct((SLAB_ROWS, 64, LANES), jnp.bfloat16),
            jax.ShapeDtypeStruct((SLAB_ROWS, 64, LANES), jnp.bfloat16),
            jax.ShapeDtypeStruct((16, LANES), jnp.int32),
        ),
        scratch_shapes=[pltpu.SemaphoreType.DMA],
        compiler_params=limit,
        cost_estimate=pl.CostEstimate(flops=200000, bytes_accessed=400000, transcendentals=0),
    )(block_tiles, block_counts.T)
    chunk = jax.ShapeDtypeStruct((devices, 1, 32, LANES), jnp.bfloat16)
    branch, view, *sends = pl.pallas_call(
        functools.partial(plan_kernel, SLAB_ROWS, NBLK // col_total),
        name="plan",
        in_specs=[vmem, anywhere],
        out_specs=(smem, vmem) + (anywhere,) * len(CAPS),
        out_shape=(jax.ShapeDtypeStruct((1,), jnp.int32), jax.ShapeDtypeStruct((6, 8, LANES), jnp.int32))
        + tuple(pltpu.HBM((devices, cap, 32, LANES), jnp.bfloat16) for cap in CAPS),
        scratch_shapes=[
            pltpu.VMEM((8, 16, LANES), jnp.int32),
            pltpu.VMEM((16, 8, LANES), jnp.int32),
            pltpu.VMEM((4, 8, LANES), jnp.int32),
            pltpu.SMEM((512,), jnp.int32),
            pltpu.SMEM((32,), jnp.int32),
            pltpu.SMEM((256,), jnp.int32),
            pltpu.VMEM((224, 64, LANES), jnp.bfloat16),
            pltpu.VMEM((224, 32, LANES), jnp.bfloat16),
            pltpu.SemaphoreType.DMA,
            pltpu.SemaphoreType.DMA,
        ],
        compiler_params=limit,
    )(meta, block_tiles)

    def applied(cap, packed):
        got = lax.all_to_all(packed, ("row", "col"), 0, 0, tiled=True)
        program, own = pl.pallas_call(
            functools.partial(route_kernel, cap),
            name="route",
            in_specs=[vmem, anywhere],
            out_specs=(smem, vmem),
            out_shape=(
                jax.ShapeDtypeStruct((PROGRAM,), jnp.int32),
                jax.ShapeDtypeStruct((OWN, 32, LANES), jnp.bfloat16),
            ),
            scratch_shapes=[
                pltpu.SMEM((4096 + 256,), jnp.int32),
                pltpu.VMEM((2, 8, LANES), jnp.int32),
                pltpu.SMEM((32,), jnp.int32),
                pltpu.SMEM((1 + OWN,), jnp.int32),
                pltpu.VMEM((OWN, 64, LANES), jnp.bfloat16),
                pltpu.SemaphoreType.DMA,
            ],
            compiler_params=limit,
            cost_estimate=pl.CostEstimate(flops=200000, bytes_accessed=400000, transcendentals=0),
        )(view, block_tiles)
        return pl.pallas_call(
            functools.partial(apply_kernel, cap),
            name="apply",
            in_specs=[anywhere, vmem, vmem, anywhere, vmem, vmem, vmem],
            out_specs=anywhere,
            out_shape=pltpu.HBM((SLAB_ROWS, 64, LANES), jnp.bfloat16),
            scratch_shapes=[
                pltpu.SMEM((PROGRAM,), jnp.int32),
                pltpu.VMEM((SLAB_ROWS, 2, 32, LANES), jnp.float32),
                pltpu.SMEM((16,), jnp.int32),
                pltpu.VMEM((SLAB_ROWS, 64, LANES), jnp.bfloat16),
                pltpu.VMEM((64, LANES), jnp.bfloat16),
                pltpu.SemaphoreType.DMA,
                pltpu.SemaphoreType.DMA((SLAB_ROWS,)),
                pltpu.SemaphoreType.DMA,
                pltpu.SemaphoreType.DMA,
            ],
            compiler_params=limit,
        )(program, got, own, block_tiles, slab, base, keep)

    branches = [functools.partial(applied, cap, packed) for cap, packed in zip(CAPS, sends)]
    return lax.switch(branch[0], branches + [lambda: dense_body(block_tiles, block_cols, block_counts)])


def solution(mesh):
    small = dict(mesh.shape) == {"row": 4, "col": 8}
    return jax.shard_map(
        sparse_body if small else dense_body,
        mesh=mesh,
        in_specs=(P("row", "col", None), P("row", "col"), P("row", "col")),
        out_specs=P("row", "col", None),
        check_vma=False,
    )
```

```python
import functools

import jax
import jax.numpy as jnp
from jax import lax
from jax.experimental import pallas as pl
from jax.experimental.pallas import tpu as pltpu
from jax.sharding import PartitionSpec as P

NBLK = 960
SLAB_ROWS = 12
LANES = 128
NONE = 1 << 30
LOCAL = 1 << 20
CAPS = (1, 2, 3, 4, 6)
OWN = 16
OWN_AT = 1 << 16
PREFIX = 1024
PROGRAM = 7168
VMEM_LIMIT = 24 << 20


def for_sending(x):
    return jax.tree.map(lambda a: a.astype(jnp.bfloat16) if a.dtype == jnp.float32 else a, x)


def passed_along(x, axis, by):
    length = lax.axis_size(axis)
    return lax.ppermute(x, axis, [(i, (i + by) % length) for i in range(length)])


def tile_products(running, visitor, first_group, panel, own_cols, own_valid, width):
    left_tiles, left_cols, left_counts = visitor
    panel_tiles, panel_cols, panel_counts = panel
    row_count = left_cols.shape[0]
    group_count = left_cols.shape[1]
    slot_count = left_cols.shape[2]
    block_size = left_tiles.shape[2]
    offset = first_group * width
    group_tiles = lax.dynamic_slice_in_dim(panel_tiles, offset, group_count * width, 0)
    group_tiles = group_tiles.reshape(group_count, width, block_size, slot_count, block_size)
    group_cols = lax.dynamic_slice_in_dim(panel_cols, offset, group_count * width, 0).reshape(
        group_count, width, slot_count
    )
    group_counts = lax.dynamic_slice_in_dim(panel_counts, offset, group_count * width, 0).reshape(
        group_count, width
    )
    group_valid = jnp.arange(slot_count, dtype=jnp.int32)[None, None, :] < group_counts[:, :, None]
    left_valid = jnp.arange(slot_count, dtype=jnp.int32)[None, None, :] < left_counts[:, :, None]
    onehot = left_cols[:, :, :, None] == jnp.arange(width, dtype=jnp.int32)[None, None, None, :]
    matched = group_cols[None, :, None, :, :, None] == own_cols[:, None, None, None, None, :]
    matched = (
        matched & group_valid[None, :, None, :, :, None] & own_valid[:, None, None, None, None, :]
    )
    matched = matched & onehot[:, :, :, :, None, None] & left_valid[:, :, :, None, None, None]
    chosen = jnp.einsum(
        "igukwv,gkywz->iguyvz",
        matched.astype(jnp.bfloat16),
        group_tiles,
        preferred_element_type=jnp.float32,
    ).astype(jnp.bfloat16)
    left_blocks = left_tiles.reshape(row_count, group_count, block_size, slot_count, block_size)
    return running + jnp.einsum(
        "igxuy,iguyvz->ixvz", left_blocks, chosen, preferred_element_type=jnp.float32
    )


def restricted_product(left_parts, panel, own_cols, own_valid):
    col_total = lax.axis_size("col")
    row_total = lax.axis_size("row")
    width = NBLK // col_total
    slab_count = own_cols.shape[0]
    slot_count = own_cols.shape[1]
    block_size = panel[0].shape[1]
    initial = jnp.zeros((slab_count, block_size, slot_count, block_size), jnp.float32)
    ratio = col_total // row_total
    row_index = lax.axis_index("row")
    col_index = lax.axis_index("col")
    moving = left_parts
    for bit_number in range(row_total.bit_length() - 1):
        arrived = jax.tree.map(
            lambda part, own: part.astype(own.dtype),
            passed_along(for_sending(moving), "col", -(ratio << bit_number)),
            moving,
        )
        flagged = row_index // (1 << bit_number) % 2 == 1

        def select_one(incoming, current):
            return jnp.where(flagged, incoming, current)

        moving = jax.tree.map(select_one, arrived, moving)
    anchor = col_index + ratio * row_index

    def advance(section_index, carried):
        running, visiting = carried
        running = tile_products(
            running,
            visiting,
            (anchor + section_index) % col_total,
            panel,
            own_cols,
            own_valid,
            width,
        )
        visiting = jax.tree.map(
            lambda part, own: part.astype(own.dtype),
            passed_along(for_sending(visiting), "col", -1),
            visiting,
        )
        return (running, visiting)

    running, moving = lax.fori_loop(0, col_total - 1, advance, (initial, moving))
    return tile_products(
        running, moving, (anchor + col_total - 1) % col_total, panel, own_cols, own_valid, width
    )


def over_rows(x):
    row_total = lax.axis_size("row")
    return lax.all_to_all(jnp.broadcast_to(x, (row_total,) + x.shape), "row", 0, 0, tiled=True)


def dense_body(block_tiles, block_cols, block_counts):
    panel_cols = over_rows(block_cols).reshape(NBLK, block_cols.shape[1])
    panel_counts = over_rows(block_counts).reshape(NBLK)
    return dense_product(
        block_tiles, panel_cols, panel_counts, block_cols[:SLAB_ROWS], block_counts[:SLAB_ROWS]
    )


def dense_product(block_tiles, panel_cols, panel_counts, own_cols, own_counts):
    block_size = block_tiles.shape[1]
    slot_count = own_cols.shape[1]
    panel_tiles = over_rows(block_tiles).reshape((NBLK,) + block_tiles.shape[1:])
    panel = (panel_tiles, panel_cols, panel_counts)
    slab_tiles = block_tiles[:SLAB_ROWS]
    own_valid = jnp.arange(slot_count, dtype=jnp.int32)[None, :] < own_counts
    first_parts = (
        slab_tiles.reshape(SLAB_ROWS, 1, block_size, slot_count * block_size),
        own_cols.reshape(SLAB_ROWS, 1, slot_count),
        own_counts,
    )
    squared = restricted_product(first_parts, panel, own_cols, own_valid)
    squared = squared.reshape(SLAB_ROWS, 1, block_size, slot_count * block_size).astype(
        jnp.bfloat16
    )
    second_parts = (squared, own_cols.reshape(SLAB_ROWS, 1, slot_count), own_counts)
    cubed = restricted_product(second_parts, panel, own_cols, own_valid)
    current = slab_tiles.reshape(SLAB_ROWS, block_size, slot_count, block_size).astype(jnp.float32)
    result = jnp.where(own_valid[:, None, :, None], 1.5 * current - 0.5 * cubed, jnp.float32(0.0))
    return result.reshape(SLAB_ROWS, block_size, slot_count * block_size).astype(jnp.bfloat16)


def lanes_of(x, index):
    return jnp.take_along_axis(x, index, axis=1)


def shr(x, n):
    return lax.shift_right_logical(x, jnp.broadcast_to(jnp.int32(n), x.shape) if jnp.ndim(n) == 0 else n)


def shl(x, n):
    return lax.shift_left(x, jnp.broadcast_to(jnp.int32(n), x.shape) if jnp.ndim(n) == 0 else n)


SEVENS = 0x77777777
EIGHTS = -(1 << 31) | 0x08888888


def capped(x):
    high = x & jnp.int32(EIGHTS)
    return (x & jnp.int32(SEVENS)) | (high - shr(high, 3))


def packed_tile(tile, high):
    tile = tile.astype(jnp.float32)
    tile = jnp.where(high > 0, pltpu.roll(tile, 64, 1), tile)
    upper = lax.broadcasted_iota(jnp.int32, (32, LANES), 1) >= 64
    return jnp.where(upper, pltpu.roll(tile[32:], 64, 1), tile[:32]).astype(jnp.bfloat16)


def show_kernel(cols_hbm, counts_hbm, out_ref, cols_ref, counts_ref, cols_sem, counts_sem):
    cols_load = pltpu.make_async_copy(cols_hbm, cols_ref, cols_sem)
    counts_load = pltpu.make_async_copy(counts_hbm, counts_ref, counts_sem)
    cols_load.start()
    counts_load.start()
    cols_load.wait()
    counts_load.wait()
    counts = counts_ref[...]
    first = jnp.where(counts > 0, cols_ref[0:1] + 1, 0)
    second = jnp.where(counts > 1, cols_ref[1:2] + 1, 0)
    out_ref[...] = jnp.broadcast_to(first | (second << 16), out_ref.shape)


def plan_kernel(rows, width, meta_ref, tiles_ref, need_ref, view_ref, *rest):
    send_refs = rest[: len(CAPS)]
    (
        part_ref, edge_ref, state_ref, list_ref, count_ref, begin_ref, fetched_ref, chunk_ref, sem, out_sem
    ) = rest[len(CAPS) :]
    r0 = lax.axis_index("row")
    c0 = lax.axis_index("col")
    lane = lax.broadcasted_iota(jnp.int32, (8, LANES), 1)
    sub = lax.broadcasted_iota(jnp.int32, (8, LANES), 0)
    slot = lane & 15
    base = lane - slot
    group = slot >> 1
    odd = slot & 1
    doubled = 2 * sub
    for r in range(4):
        for c in range(8):
            piece = meta_ref[8 * r + c]
            part_ref[2 * r, c : c + 1, :] = piece[:, :LANES]
            part_ref[2 * r + 1, c : c + 1, : piece.shape[1] - LANES] = piece[:, LANES:]
    parts = [part_ref[j] for j in range(8)]
    for r in range(4):
        for half in range(2):
            i8 = (lane >> 4) + 8 * half
            own = jnp.where(i8 < rows, lanes_of(parts[2 * r], i8), 0)
            col = jnp.sum(jnp.where(sub == group, own, 0), axis=0, keepdims=True)
            col = shr(col, 16 * odd[:1]) & 0xFFFF
            k = group[:1] * width + col - 1
            rk = (k >= 240).astype(jnp.int32) + (k >= 480).astype(jnp.int32) + (k >= 720).astype(jnp.int32)
            n = k - 240 * rk
            where_k = jnp.where(col > 0, 2 * rk + (n >> 7), -1)
            at = jnp.broadcast_to(n & (LANES - 1), (8, LANES))
            piece_k = jnp.broadcast_to(where_k, (8, LANES))
            found = jnp.zeros((8, LANES), jnp.int32)
            for j in range(8):
                found = jnp.where(piece_k == j, lanes_of(parts[j], at), found)
            b0 = own & 0xFFFF
            b1 = shr(own, 16)
            g0 = found & 0xFFFF
            g1 = shr(found, 16)
            at0 = (b0 > 0) & (g0 == b0)
            at0_high = (b0 > 0) & (g1 == b0)
            at1 = (b1 > 0) & (g0 == b1)
            at1_high = (b1 > 0) & (g1 == b1)
            high = jnp.where(at0_high, 1, 0) | jnp.where(at1_high, 2, 0)
            any_edge = jnp.where(at0, 1, 0) | jnp.where(at1, 2, 0) | high
            s = 2 * r + half
            state_ref[0, s : s + 1, :] = jnp.sum(shl(any_edge, doubled), axis=0, keepdims=True)
            state_ref[1, s : s + 1, :] = jnp.sum(shl(high, doubled), axis=0, keepdims=True)
            state_ref[2, s : s + 1, :] = jnp.where(col > 0, k, -1)
    out = state_ref[0]
    which = state_ref[1]
    k = state_ref[2]
    rk = (k >= 240).astype(jnp.int32) + (k >= 480).astype(jnp.int32) + (k >= 720).astype(jnp.int32)
    rsub = sub >> 1
    row = (sub & 1) * 8 + (lane >> 4)

    into = jnp.zeros_like(out)
    for a in range(16):
        into = into | shl(shr(lanes_of(out, base + a), slot) & 1, a)
    spread = (out | shr(out, 1)) & 0x5555
    spread = (spread | shl(spread, 8)) & 0x00FF00FF
    spread = (spread | shl(spread, 4)) & 0x0F0F0F0F
    spread = (spread | shl(spread, 2)) & 0x11111111
    itself = rsub * 240 + row
    on_diag = (k == itself) & (k >= 0)
    first_slot = 2 * (rsub * (240 // width))
    diag = jnp.full_like(slot, -1)
    for v in range(2):
        held = lanes_of(k, base + first_slot + v)
        diag = jnp.where((held == itself) & (held >= 0), first_slot + v, diag)
    has_diag = diag >= 0
    diag_at = base + jnp.maximum(diag, 0)
    left = jnp.zeros_like(out)
    extra = jnp.zeros_like(out)
    edges = []
    for b in range(16):
        has = (shr(out, b) & 1) > 0
        heads = lanes_of(spread, base + b)
        left = left | jnp.where(has, heads, 0)
        edge = jnp.where(has, heads | jnp.where(into != 0, 1 << (4 * (b // 2)), 0), 0)
        extra = extra | jnp.where((slot == b) & has_diag, lanes_of(edge, diag_at), 0)
        edges.append(jnp.where(on_diag, 0, edge))
    left = left | extra

    fifteen = jnp.full_like(out, 15)
    sent_left = left & ~shl(fifteen, 4 * (slot >> 1))
    sent = []
    bits = jnp.where((shr(left, 4 * c0) & 1) > 0, 1 << 16, 0)
    for b in range(16):
        own_nibble = (15 << (4 * (b // 2))) if b < 14 else -(1 << 28)
        sent.append(edges[b] & ~jnp.where(rk == rsub, jnp.int32(own_nibble), 0))
        edge_ref[b] = sent[b]
        bits = bits | jnp.where((shr(edges[b], 4 * c0) & 1) > 0, 1 << b, 0)

    mine = rsub == r0
    view_ref[0] = jnp.where(mine, bits, 0)
    view_ref[1] = jnp.where(mine & (into != 0), shr(out, 2 * c0) & 3, 0)
    view_ref[2] = into
    view_ref[3] = which
    view_ref[4] = k
    view_ref[5] = diag

    from_left = jnp.where(mine & ((slot >> 1) == c0), sent_left, 0)
    from_rows = [jnp.where(rk == r0, edge_ref[2 * c0 + v], 0) for v in range(2)]
    masks = [from_left] + from_rows
    place = sub * LANES + lane
    busy = jnp.where((masks[0] | masks[1] | masks[2]) != 0, place, NONE)
    state_ref[3] = busy
    for d in range(32):
        count_ref[d] = 0
    local = k - 240 * r0

    def pick(x, hit):
        return jnp.sum(jnp.where(hit, x, 0))

    def send_from(carried):
        spot, fetched, total = carried
        hit = place == spot
        left_over = jnp.where(hit, NONE, state_ref[3])
        state_ref[3] = left_over
        following = jnp.min(left_over)
        r = lax.shift_right_logical(spot, 8)
        picked_which = pick(which, hit)
        picked_row = pick(local, hit)
        picked = [pick(mask, hit) for mask in masks]
        slab_row = (lax.shift_right_logical(spot, 7) & 1) * 8 + (lax.shift_right_logical(spot, 4) & 7)
        sources = [
            2 * slab_row + (spot & 1),
            2 * picked_row + (lax.shift_right_logical(picked_which, 2 * c0) & 1),
            2 * picked_row + (lax.shift_right_logical(picked_which, 2 * c0 + 1) & 1),
        ]
        for source, nibbles in zip(sources, picked):

            def to_groups(carried):
                fetched, total = carried
                pltpu.make_async_copy(tiles_ref.at[source >> 1], fetched_ref.at[fetched], sem).start()
                begin_ref[fetched] = total
                for g in range(8):
                    on = lax.shift_right_logical(nibbles, 4 * g) & 1
                    d = r * 8 + g
                    seen = count_ref[d]
                    list_ref[2 * total] = seen * 32 + d
                    list_ref[2 * total + 1] = source
                    count_ref[d] = seen + on
                    total = total + on
                return fetched + 1, total

            fetched, total = lax.cond(nibbles != 0, to_groups, lambda t: t, (fetched, total))
        return following, fetched, total

    first_spot = jnp.min(busy)
    _, fetched, total = lax.while_loop(
        lambda s: (s[0] < NONE) & (s[2] < 31 * CAPS[-1]), send_from, (first_spot, jnp.int32(0), jnp.int32(0))
    )
    words = []
    for p in range(8):
        pair = sent[2 * p] + sent[2 * p + 1]
        for r in range(4):
            words.append(jnp.where(rk == r, pair, 0))
    span = LANES // 2
    while len(words) > 1:
        if len(words) == 8:
            words = [capped(x) for x in words]
        merged = []
        first = (lane & span) == 0
        for x, y in zip(words[0::2], words[1::2]):
            z = jnp.where(first, x, y) + lanes_of(jnp.where(first, y, x), lane ^ span)
            merged.append(z if len(words) > 8 else capped(z))
        words = merged
        span //= 2
    word = words[0]
    while span >= 1:
        word = capped(word + lanes_of(word, lane ^ span))
        span //= 2
    by_slot = sent_left + lanes_of(sent_left, lane ^ 1)
    by_slot = by_slot + lanes_of(by_slot, lane ^ 64)
    by_slot = capped(by_slot + lanes_of(by_slot, lane ^ 32))
    by_slot = capped(by_slot + lanes_of(by_slot, lane ^ 16))
    group = (shr(lane, 4) & 1) | (shr(lane, 2) & 2) | (lane & 4)
    from_row = (shr(lane, 6) & 1) | (shr(lane, 4) & 2)
    word = capped(word + jnp.where(from_row == rsub, lanes_of(by_slot, 2 * group), 0))
    word = capped(word + pltpu.roll(word, 7, 0))
    most = jnp.zeros_like(word)
    for g in range(8):
        most = jnp.maximum(most, shr(word, 4 * g) & 15)
    most = jnp.where((sub & 1) == 0, most, 0)
    needed = jnp.max(most)
    chosen = jnp.int32(0)
    for cap in CAPS:
        chosen = chosen + (needed > cap).astype(jnp.int32)
    need_ref[0] = chosen
    begin_ref[fetched] = total

    @pl.loop(0, fetched)
    def _(n):
        pltpu.make_async_copy(tiles_ref.at[0], fetched_ref.at[n], sem).wait()

    @pl.loop(0, fetched)
    def _(n):
        chunk_ref[n] = packed_tile(fetched_ref[n], list_ref[2 * begin_ref[n] + 1] & 1)

    for index, send_ref in enumerate(send_refs):

        @pl.when((chosen == index) & (total > 0))
        def _(send_ref=send_ref):
            @pl.loop(0, fetched)
            def _(n):
                @pl.loop(begin_ref[n], begin_ref[n + 1])
                def _(t):
                    to = list_ref[2 * t]
                    pltpu.make_async_copy(chunk_ref.at[n], send_ref.at[to & 31, to >> 5], out_sem).start()

            @pl.loop(0, total)
            def _(t):
                pltpu.make_async_copy(chunk_ref.at[0], send_ref.at[0, 0], out_sem).wait()


def route_kernel(
    cap,
    view_ref,
    tiles_ref,
    program_ref,
    own_ref,
    slab_ref,
    base_ref,
    keep_ref,
    place_ref,
    state_ref,
    count_ref,
    kept_ref,
    fetched_ref,
    sem,
    slab_sem,
):
    slab_load = pltpu.make_async_copy(tiles_ref.at[:SLAB_ROWS], slab_ref, slab_sem)
    slab_load.start()
    r0 = lax.axis_index("row")
    c0 = lax.axis_index("col")
    me = r0 * 8 + c0
    lane = lax.broadcasted_iota(jnp.int32, (8, LANES), 1)
    sub = lax.broadcasted_iota(jnp.int32, (8, LANES), 0)
    place = sub * LANES + lane
    bits = view_ref[0]
    heads = view_ref[1]
    into = view_ref[2]
    which = view_ref[3]
    k = view_ref[4]
    diag = view_ref[5]
    for d in range(32):
        count_ref[d] = 0
    kept_ref[0] = 0

    def pick(x, hit):
        return jnp.sum(jnp.where(hit, x, 0))

    state_ref[0] = jnp.where(bits != 0, place, NONE)

    def arrive(spot):
        hit = place == spot
        left_over = jnp.where(hit, NONE, state_ref[0])
        state_ref[0] = left_over
        following = jnp.min(left_over)
        at = spot - 256 * r0
        picked = pick(bits, hit)
        picked_k = pick(k, hit)
        picked_which = pick(which, hit)
        source_row = picked_k // 240

        def put(entry, source, held_at):
            @pl.when(source == me)
            def _():
                kept = kept_ref[0]
                place_ref[entry] = jnp.where(kept < OWN, OWN_AT + kept, LOCAL + held_at)

                @pl.when(kept < OWN)
                def _():
                    pltpu.make_async_copy(tiles_ref.at[held_at >> 1], fetched_ref.at[kept], sem).start()
                    kept_ref[0] = kept + 1
                    kept_ref[1 + kept] = held_at

            @pl.when(source != me)
            def _():
                place_ref[entry] = source * cap + count_ref[source]
                count_ref[source] = count_ref[source] + 1

        @pl.when((picked >> 16) > 0)
        def _():
            put(4096 + at, r0 * 8 + ((at & 15) >> 1), 2 * (at >> 4) + (at & 1))

        @pl.loop(0, 16)
        def _(b):
            @pl.when(((picked >> b) & 1) > 0)
            def _():
                put(
                    at * 16 + b,
                    source_row * 8 + (b >> 1),
                    2 * (picked_k - 240 * source_row) + ((picked_which >> b) & 1),
                )

        return following

    lax.while_loop(lambda s: s < NONE, arrive, jnp.min(state_ref[0]))
    state_ref[1] = jnp.where(heads != 0, place, NONE)

    def follow(carried):
        spot, head_count, p = carried
        hit = place == spot
        left_over = jnp.where(hit, NONE, state_ref[1])
        state_ref[1] = left_over
        following = jnp.min(left_over)
        at = spot - 256 * r0
        i = at >> 4
        b = at & 15
        tails = pick(into, hit)
        ends = pick(heads, hit)
        self_slot = pick(diag, hit)
        program_ref[p] = i
        for v in range(2):
            c = 2 * c0 + v
            entry = jnp.where(b == self_slot, 4096 + i * 16 + c, at * 16 + c)
            program_ref[p + 2 + v] = jnp.where(((ends >> v) & 1) > 0, place_ref[entry], -1)

        def tail(a, count):
            on = (tails >> a) & 1

            @pl.when(on > 0)
            def _():
                q = p + 4 + 2 * count
                program_ref[q] = place_ref[4096 + i * 16 + a]
                program_ref[q + 1] = place_ref[
                    jnp.where(a == self_slot, 4096 + i * 16 + b, (i * 16 + a) * 16 + b)
                ]

            return count + on

        count = lax.fori_loop(0, 16, tail, jnp.int32(0))
        program_ref[p + 1] = count
        return following, head_count + 1, p + 4 + 2 * count

    _, head_count, end = lax.while_loop(
        lambda s: s[0] < NONE, follow, (jnp.min(state_ref[1]), jnp.int32(0), jnp.int32(2))
    )
    program_ref[0] = head_count
    program_ref[1] = end
    own_slot = 16 * sub + 2 * c0 + (lane >= 64).astype(jnp.int32)
    for half in range(2):
        held = jnp.broadcast_to(view_ref[4, pl.ds(2 * r0 + half, 1), :], (8, LANES))
        keep_ref[8 * half : 8 * half + 8, :] = (lanes_of(held, own_slot) >= 0).astype(jnp.int32)
    slab_load.wait()
    for i in range(SLAB_ROWS):
        keep = jnp.broadcast_to(keep_ref[i : i + 1, :], (64, LANES)) > 0
        base_ref[i] = jnp.where(keep, 1.5 * slab_ref[i].astype(jnp.float32), 0.0).astype(jnp.bfloat16)
    kept = kept_ref[0]

    @pl.loop(0, kept)
    def _(n):
        pltpu.make_async_copy(tiles_ref.at[0], fetched_ref.at[n], sem).wait()

    @pl.loop(0, kept)
    def _(n):
        own_ref[n] = packed_tile(fetched_ref[n], kept_ref[1 + n] & 1)


def apply_kernel(
    cap,
    program_hbm,
    got_ref,
    own_ref,
    tiles_ref,
    slab_ref,
    base_ref,
    keep_ref,
    out_ref,
    program_ref,
    cube_ref,
    touched_ref,
    patch_ref,
    spare_ref,
    sem,
    patch_sem,
    spare_sem,
    program_sem,
):
    load = pltpu.make_async_copy(program_hbm.at[:PREFIX], program_ref.at[:PREFIX], program_sem)
    load.start()
    write = pltpu.make_async_copy(base_ref, out_ref, sem)
    write.start()
    for i in range(SLAB_ROWS):
        touched_ref[i] = 0
    low = lax.broadcasted_iota(jnp.int32, (32, LANES), 1) < 64
    load.wait()

    @pl.when(program_ref[1] > PREFIX)
    def _():
        rest = pltpu.make_async_copy(program_hbm, program_ref, program_sem)
        rest.start()
        rest.wait()

    def tile_at(where):
        def near():
            got_at = jnp.minimum(where, 32 * cap - 1)
            own_at = jnp.clip(where - OWN_AT, 0, OWN - 1)
            return jnp.where(where < OWN_AT, got_ref[got_at // cap, got_at % cap], own_ref[own_at])

        def far():
            copy = pltpu.make_async_copy(tiles_ref.at[(where - LOCAL) >> 1], spare_ref, spare_sem)
            copy.start()
            copy.wait()
            return packed_tile(spare_ref[...], where & 1)

        return lax.cond(where < LOCAL, near, far)

    def twice(tile):
        x = tile.astype(jnp.float32)
        y = pltpu.roll(x, 64, 1)
        zero = jnp.zeros_like(x)
        return jnp.concatenate(
            [jnp.where(low, x, zero), jnp.where(low, y, zero), jnp.where(low, zero, y), jnp.where(low, zero, x)], 0
        ).astype(jnp.bfloat16)

    def product(x, y):
        return jnp.dot(x, twice(y), preferred_element_type=jnp.float32)

    def head(_, p):
        i = program_ref[p]
        count = program_ref[p + 1]

        def tail(t, total):
            q = p + 4 + 2 * t
            return total + product(tile_at(program_ref[q]), tile_at(program_ref[q + 1]))

        total = lax.fori_loop(0, count, tail, jnp.zeros((32, LANES), jnp.float32))
        squared = total.astype(jnp.bfloat16)

        @pl.when(touched_ref[i] == 0)
        def _():
            touched_ref[i] = 1
            cube_ref[i] = jnp.zeros((2, 32, LANES), jnp.float32)

        for v in range(2):
            where = program_ref[p + 2 + v]

            @pl.when(where >= 0)
            def _():
                cube_ref[i, v] += product(squared, tile_at(where))

        return p + 4 + 2 * count

    lax.fori_loop(0, program_ref[0], head, jnp.int32(2))
    write.wait()

    def patch(i):
        return pltpu.make_async_copy(patch_ref.at[i], out_ref.at[i], patch_sem.at[i])

    @pl.loop(0, SLAB_ROWS)
    def _(i):
        @pl.when(touched_ref[i] > 0)
        def _():
            x = cube_ref[i, 0]
            y = cube_ref[i, 1]
            cubed = jnp.concatenate(
                [jnp.where(low, x, pltpu.roll(y, 64, 1)), jnp.where(low, pltpu.roll(x, 64, 1), y)], 0
            )
            keep = jnp.broadcast_to(keep_ref[pl.ds(i, 1), :], (64, LANES)) > 0
            current = slab_ref[i].astype(jnp.float32)
            patch_ref[i] = jnp.where(keep, 1.5 * current - 0.5 * cubed, 0.0).astype(jnp.bfloat16)
            patch(i).start()

    @pl.loop(0, SLAB_ROWS)
    def _(i):
        @pl.when(touched_ref[i] > 0)
        def _():
            patch(i).wait()


def sparse_body(block_tiles, block_cols, block_counts):
    row_total = lax.axis_size("row")
    col_total = lax.axis_size("col")
    devices = row_total * col_total
    per_device = block_cols.shape[0]
    shown = pl.pallas_call(
        show_kernel,
        name="show",
        in_specs=[pl.BlockSpec(memory_space=pl.ANY)] * 2,
        out_shape=jax.ShapeDtypeStruct((devices, 1, per_device), jnp.int32),
        scratch_shapes=[
            pltpu.VMEM((2, per_device), jnp.int32),
            pltpu.VMEM((1, per_device), jnp.int32),
            pltpu.SemaphoreType.DMA,
            pltpu.SemaphoreType.DMA,
        ],
        compiler_params=pltpu.CompilerParams(vmem_limit_bytes=VMEM_LIMIT),
    )(
        pltpu.with_memory_space_constraint(block_cols.T, pltpu.HBM),
        pltpu.with_memory_space_constraint(block_counts.T, pltpu.HBM),
    )
    meta = lax.all_to_all(shown, ("row", "col"), 0, 0, tiled=True)
    vmem = pl.BlockSpec(memory_space=pltpu.VMEM)
    smem = pl.BlockSpec(memory_space=pltpu.SMEM)
    anywhere = pl.BlockSpec(memory_space=pl.ANY)
    limit = pltpu.CompilerParams(vmem_limit_bytes=VMEM_LIMIT)
    branch, view, *sends = pl.pallas_call(
        functools.partial(plan_kernel, SLAB_ROWS, NBLK // col_total),
        name="plan",
        in_specs=[vmem, anywhere],
        out_specs=(smem, vmem) + (anywhere,) * len(CAPS),
        out_shape=(pltpu.SMEM((1,), jnp.int32), jax.ShapeDtypeStruct((6, 8, LANES), jnp.int32))
        + tuple(pltpu.HBM((devices, cap, 32, LANES), jnp.bfloat16) for cap in CAPS),
        scratch_shapes=[
            pltpu.VMEM((8, 8, LANES), jnp.int32),
            pltpu.VMEM((16, 8, LANES), jnp.int32),
            pltpu.VMEM((4, 8, LANES), jnp.int32),
            pltpu.SMEM((512,), jnp.int32),
            pltpu.SMEM((32,), jnp.int32),
            pltpu.SMEM((256,), jnp.int32),
            pltpu.VMEM((248, 64, LANES), jnp.bfloat16),
            pltpu.VMEM((248, 32, LANES), jnp.bfloat16),
            pltpu.SemaphoreType.DMA,
            pltpu.SemaphoreType.DMA,
        ],
        compiler_params=limit,
    )(meta, block_tiles)

    def applied(cap, packed):
        got = lax.all_to_all(packed, ("row", "col"), 0, 0, tiled=True)
        program, own, slab, base, keep = pl.pallas_call(
            functools.partial(route_kernel, cap),
            name="route",
            in_specs=[vmem, anywhere],
            out_specs=(smem, vmem, vmem, vmem, vmem),
            out_shape=(
                jax.ShapeDtypeStruct((PROGRAM,), jnp.int32),
                jax.ShapeDtypeStruct((OWN, 32, LANES), jnp.bfloat16),
                jax.ShapeDtypeStruct((SLAB_ROWS, 64, LANES), jnp.bfloat16),
                jax.ShapeDtypeStruct((SLAB_ROWS, 64, LANES), jnp.bfloat16),
                jax.ShapeDtypeStruct((16, LANES), jnp.int32),
            ),
            scratch_shapes=[
                pltpu.SMEM((4096 + 256,), jnp.int32),
                pltpu.VMEM((2, 8, LANES), jnp.int32),
                pltpu.SMEM((32,), jnp.int32),
                pltpu.SMEM((1 + OWN,), jnp.int32),
                pltpu.VMEM((OWN, 64, LANES), jnp.bfloat16),
                pltpu.SemaphoreType.DMA,
                pltpu.SemaphoreType.DMA,
            ],
            compiler_params=limit,
            cost_estimate=pl.CostEstimate(flops=200000, bytes_accessed=400000, transcendentals=0),
        )(view, block_tiles)
        return pl.pallas_call(
            functools.partial(apply_kernel, cap),
            name="apply",
            in_specs=[anywhere, vmem, vmem, anywhere, vmem, vmem, vmem],
            out_specs=anywhere,
            out_shape=pltpu.HBM((SLAB_ROWS, 64, LANES), jnp.bfloat16),
            scratch_shapes=[
                pltpu.SMEM((PROGRAM,), jnp.int32),
                pltpu.VMEM((SLAB_ROWS, 2, 32, LANES), jnp.float32),
                pltpu.SMEM((16,), jnp.int32),
                pltpu.VMEM((SLAB_ROWS, 64, LANES), jnp.bfloat16),
                pltpu.VMEM((64, LANES), jnp.bfloat16),
                pltpu.SemaphoreType.DMA,
                pltpu.SemaphoreType.DMA((SLAB_ROWS,)),
                pltpu.SemaphoreType.DMA,
                pltpu.SemaphoreType.DMA,
            ],
            compiler_params=limit,
        )(program, got, own, block_tiles, slab, base, keep)

    branches = [functools.partial(applied, cap, packed) for cap, packed in zip(CAPS, sends)]

    def dense():
        own_group = meta.reshape(row_total, col_total, per_device)[:, lax.axis_index("col")].reshape(NBLK)
        pair = jnp.stack([own_group & 0xFFFF, own_group >> 16], axis=1)
        counts = jnp.sum((pair > 0).astype(jnp.int32), axis=1)
        start = lax.axis_index("row") * per_device
        own = lax.dynamic_slice_in_dim(pair, start, SLAB_ROWS, 0) - 1
        own_counts = lax.dynamic_slice_in_dim(counts, start, SLAB_ROWS, 0)[:, None]
        return dense_product(block_tiles, pair - 1, counts, own, own_counts)

    return lax.switch(branch[0], branches + [dense])


def solution(mesh):
    small = dict(mesh.shape) == {"row": 4, "col": 8}
    return jax.shard_map(
        sparse_body if small else dense_body,
        mesh=mesh,
        in_specs=(P("row", "col", None), P("row", "col"), P("row", "col")),
        out_specs=P("row", "col", None),
        check_vma=False,
    )
```

```python
import functools

import jax
import jax.numpy as jnp
from jax import lax
from jax.experimental import pallas as pl
from jax.experimental.pallas import tpu as pltpu
from jax.sharding import PartitionSpec as P

NBLK = 960
SLAB_ROWS = 12
LANES = 128
NONE = 1 << 30
LOCAL = 1 << 20
CAPS = (1, 2, 3, 4, 6)
OWN = 16
OWN_AT = 1 << 16
PREFIX = 1024
PROGRAM = 7168
VMEM_LIMIT = 24 << 20


def for_sending(x):
    return jax.tree.map(lambda a: a.astype(jnp.bfloat16) if a.dtype == jnp.float32 else a, x)


def passed_along(x, axis, by):
    length = lax.axis_size(axis)
    return lax.ppermute(x, axis, [(i, (i + by) % length) for i in range(length)])


def tile_products(running, visitor, first_group, panel, own_cols, own_valid, width):
    left_tiles, left_cols, left_counts = visitor
    panel_tiles, panel_cols, panel_counts = panel
    row_count = left_cols.shape[0]
    group_count = left_cols.shape[1]
    slot_count = left_cols.shape[2]
    block_size = left_tiles.shape[2]
    offset = first_group * width
    group_tiles = lax.dynamic_slice_in_dim(panel_tiles, offset, group_count * width, 0)
    group_tiles = group_tiles.reshape(group_count, width, block_size, slot_count, block_size)
    group_cols = lax.dynamic_slice_in_dim(panel_cols, offset, group_count * width, 0).reshape(
        group_count, width, slot_count
    )
    group_counts = lax.dynamic_slice_in_dim(panel_counts, offset, group_count * width, 0).reshape(
        group_count, width
    )
    group_valid = jnp.arange(slot_count, dtype=jnp.int32)[None, None, :] < group_counts[:, :, None]
    left_valid = jnp.arange(slot_count, dtype=jnp.int32)[None, None, :] < left_counts[:, :, None]
    onehot = left_cols[:, :, :, None] == jnp.arange(width, dtype=jnp.int32)[None, None, None, :]
    matched = group_cols[None, :, None, :, :, None] == own_cols[:, None, None, None, None, :]
    matched = (
        matched & group_valid[None, :, None, :, :, None] & own_valid[:, None, None, None, None, :]
    )
    matched = matched & onehot[:, :, :, :, None, None] & left_valid[:, :, :, None, None, None]
    chosen = jnp.einsum(
        "igukwv,gkywz->iguyvz",
        matched.astype(jnp.bfloat16),
        group_tiles,
        preferred_element_type=jnp.float32,
    ).astype(jnp.bfloat16)
    left_blocks = left_tiles.reshape(row_count, group_count, block_size, slot_count, block_size)
    return running + jnp.einsum(
        "igxuy,iguyvz->ixvz", left_blocks, chosen, preferred_element_type=jnp.float32
    )


def restricted_product(left_parts, panel, own_cols, own_valid):
    col_total = lax.axis_size("col")
    row_total = lax.axis_size("row")
    width = NBLK // col_total
    slab_count = own_cols.shape[0]
    slot_count = own_cols.shape[1]
    block_size = panel[0].shape[1]
    initial = jnp.zeros((slab_count, block_size, slot_count, block_size), jnp.float32)
    ratio = col_total // row_total
    row_index = lax.axis_index("row")
    col_index = lax.axis_index("col")
    moving = left_parts
    for bit_number in range(row_total.bit_length() - 1):
        arrived = jax.tree.map(
            lambda part, own: part.astype(own.dtype),
            passed_along(for_sending(moving), "col", -(ratio << bit_number)),
            moving,
        )
        flagged = row_index // (1 << bit_number) % 2 == 1

        def select_one(incoming, current):
            return jnp.where(flagged, incoming, current)

        moving = jax.tree.map(select_one, arrived, moving)
    anchor = col_index + ratio * row_index

    def advance(section_index, carried):
        running, visiting = carried
        running = tile_products(
            running,
            visiting,
            (anchor + section_index) % col_total,
            panel,
            own_cols,
            own_valid,
            width,
        )
        visiting = jax.tree.map(
            lambda part, own: part.astype(own.dtype),
            passed_along(for_sending(visiting), "col", -1),
            visiting,
        )
        return (running, visiting)

    running, moving = lax.fori_loop(0, col_total - 1, advance, (initial, moving))
    return tile_products(
        running, moving, (anchor + col_total - 1) % col_total, panel, own_cols, own_valid, width
    )


def over_rows(x):
    row_total = lax.axis_size("row")
    return lax.all_to_all(jnp.broadcast_to(x, (row_total,) + x.shape), "row", 0, 0, tiled=True)


def dense_body(block_tiles, block_cols, block_counts):
    panel_cols = over_rows(block_cols).reshape(NBLK, block_cols.shape[1])
    panel_counts = over_rows(block_counts).reshape(NBLK)
    return dense_product(
        block_tiles, panel_cols, panel_counts, block_cols[:SLAB_ROWS], block_counts[:SLAB_ROWS]
    )


def dense_product(block_tiles, panel_cols, panel_counts, own_cols, own_counts):
    block_size = block_tiles.shape[1]
    slot_count = own_cols.shape[1]
    panel_tiles = over_rows(block_tiles).reshape((NBLK,) + block_tiles.shape[1:])
    panel = (panel_tiles, panel_cols, panel_counts)
    slab_tiles = block_tiles[:SLAB_ROWS]
    own_valid = jnp.arange(slot_count, dtype=jnp.int32)[None, :] < own_counts
    first_parts = (
        slab_tiles.reshape(SLAB_ROWS, 1, block_size, slot_count * block_size),
        own_cols.reshape(SLAB_ROWS, 1, slot_count),
        own_counts,
    )
    squared = restricted_product(first_parts, panel, own_cols, own_valid)
    squared = squared.reshape(SLAB_ROWS, 1, block_size, slot_count * block_size).astype(
        jnp.bfloat16
    )
    second_parts = (squared, own_cols.reshape(SLAB_ROWS, 1, slot_count), own_counts)
    cubed = restricted_product(second_parts, panel, own_cols, own_valid)
    current = slab_tiles.reshape(SLAB_ROWS, block_size, slot_count, block_size).astype(jnp.float32)
    result = jnp.where(own_valid[:, None, :, None], 1.5 * current - 0.5 * cubed, jnp.float32(0.0))
    return result.reshape(SLAB_ROWS, block_size, slot_count * block_size).astype(jnp.bfloat16)


def lanes_of(x, index):
    return jnp.take_along_axis(x, index, axis=1)


def shr(x, n):
    return lax.shift_right_logical(x, jnp.broadcast_to(jnp.int32(n), x.shape) if jnp.ndim(n) == 0 else n)


def shl(x, n):
    return lax.shift_left(x, jnp.broadcast_to(jnp.int32(n), x.shape) if jnp.ndim(n) == 0 else n)


SEVENS = 0x77777777
EIGHTS = -(1 << 31) | 0x08888888


def capped(x):
    high = x & jnp.int32(EIGHTS)
    return (x & jnp.int32(SEVENS)) | (high - shr(high, 3))


def packed_tile(tile, high):
    tile = tile.astype(jnp.float32)
    tile = jnp.where(high > 0, pltpu.roll(tile, 64, 1), tile)
    upper = lax.broadcasted_iota(jnp.int32, (32, LANES), 1) >= 64
    return jnp.where(upper, pltpu.roll(tile[32:], 64, 1), tile[:32]).astype(jnp.bfloat16)


def show_kernel(cols_hbm, counts_hbm, out_ref, cols_ref, counts_ref, cols_sem, counts_sem):
    cols_load = pltpu.make_async_copy(cols_hbm, cols_ref, cols_sem)
    counts_load = pltpu.make_async_copy(counts_hbm, counts_ref, counts_sem)
    cols_load.start()
    counts_load.start()
    cols_load.wait()
    counts_load.wait()
    counts = counts_ref[...]
    first = jnp.where(counts > 0, cols_ref[0:1] + 1, 0)
    second = jnp.where(counts > 1, cols_ref[1:2] + 1, 0)
    out_ref[...] = jnp.broadcast_to(first | (second << 16), out_ref.shape)


def plan_kernel(rows, width, meta_ref, tiles_ref, need_ref, view_ref, *rest):
    send_refs = rest[: len(CAPS)]
    (
        part_ref, edge_ref, state_ref, list_ref, count_ref, begin_ref, fetched_ref, chunk_ref, sem, out_sem
    ) = rest[len(CAPS) :]
    r0 = lax.axis_index("row")
    c0 = lax.axis_index("col")
    lane = lax.broadcasted_iota(jnp.int32, (8, LANES), 1)
    sub = lax.broadcasted_iota(jnp.int32, (8, LANES), 0)
    slot = lane & 15
    base = lane - slot
    group = slot >> 1
    odd = slot & 1
    doubled = 2 * sub
    for r in range(4):
        for c in range(8):
            piece = meta_ref[8 * r + c]
            part_ref[2 * r, c : c + 1, :] = piece[:, :LANES]
            part_ref[2 * r + 1, c : c + 1, : piece.shape[1] - LANES] = piece[:, LANES:]
    parts = [part_ref[j] for j in range(8)]
    for r in range(4):
        for half in range(2):
            i8 = (lane >> 4) + 8 * half
            own = jnp.where(i8 < rows, lanes_of(parts[2 * r], i8), 0)
            col = jnp.sum(jnp.where(sub == group, own, 0), axis=0, keepdims=True)
            col = shr(col, 16 * odd[:1]) & 0xFFFF
            k = group[:1] * width + col - 1
            rk = (k >= 240).astype(jnp.int32) + (k >= 480).astype(jnp.int32) + (k >= 720).astype(jnp.int32)
            n = k - 240 * rk
            where_k = jnp.where(col > 0, 2 * rk + (n >> 7), -1)
            at = jnp.broadcast_to(n & (LANES - 1), (8, LANES))
            piece_k = jnp.broadcast_to(where_k, (8, LANES))
            found = jnp.zeros((8, LANES), jnp.int32)
            for j in range(8):
                found = jnp.where(piece_k == j, lanes_of(parts[j], at), found)
            b0 = own & 0xFFFF
            b1 = shr(own, 16)
            g0 = found & 0xFFFF
            g1 = shr(found, 16)
            at0 = (b0 > 0) & (g0 == b0)
            at0_high = (b0 > 0) & (g1 == b0)
            at1 = (b1 > 0) & (g0 == b1)
            at1_high = (b1 > 0) & (g1 == b1)
            high = jnp.where(at0_high, 1, 0) | jnp.where(at1_high, 2, 0)
            any_edge = jnp.where(at0, 1, 0) | jnp.where(at1, 2, 0) | high
            s = 2 * r + half
            state_ref[0, s : s + 1, :] = jnp.sum(shl(any_edge, doubled), axis=0, keepdims=True)
            state_ref[1, s : s + 1, :] = jnp.sum(shl(high, doubled), axis=0, keepdims=True)
            state_ref[2, s : s + 1, :] = jnp.where(col > 0, k, -1)
    out = state_ref[0]
    which = state_ref[1]
    k = state_ref[2]
    rk = (k >= 240).astype(jnp.int32) + (k >= 480).astype(jnp.int32) + (k >= 720).astype(jnp.int32)
    rsub = sub >> 1
    row = (sub & 1) * 8 + (lane >> 4)

    into = jnp.zeros_like(out)
    for a in range(16):
        into = into | shl(shr(lanes_of(out, base + a), slot) & 1, a)
    spread = (out | shr(out, 1)) & 0x5555
    spread = (spread | shl(spread, 8)) & 0x00FF00FF
    spread = (spread | shl(spread, 4)) & 0x0F0F0F0F
    spread = (spread | shl(spread, 2)) & 0x11111111
    itself = rsub * 240 + row
    on_diag = (k == itself) & (k >= 0)
    first_slot = 2 * (rsub * (240 // width))
    diag = jnp.full_like(slot, -1)
    for v in range(2):
        held = lanes_of(k, base + first_slot + v)
        diag = jnp.where((held == itself) & (held >= 0), first_slot + v, diag)
    has_diag = diag >= 0
    diag_at = base + jnp.maximum(diag, 0)
    left = jnp.zeros_like(out)
    extra = jnp.zeros_like(out)
    edges = []
    for b in range(16):
        has = (shr(out, b) & 1) > 0
        heads = lanes_of(spread, base + b)
        left = left | jnp.where(has, heads, 0)
        edge = jnp.where(has, heads | jnp.where(into != 0, 1 << (4 * (b // 2)), 0), 0)
        extra = extra | jnp.where((slot == b) & has_diag, lanes_of(edge, diag_at), 0)
        edges.append(jnp.where(on_diag, 0, edge))
    left = left | extra

    fifteen = jnp.full_like(out, 15)
    sent_left = left & ~shl(fifteen, 4 * (slot >> 1))
    sent = []
    bits = jnp.where((shr(left, 4 * c0) & 1) > 0, 1 << 16, 0)
    for b in range(16):
        own_nibble = (15 << (4 * (b // 2))) if b < 14 else -(1 << 28)
        sent.append(edges[b] & ~jnp.where(rk == rsub, jnp.int32(own_nibble), 0))
        edge_ref[b] = sent[b]
        bits = bits | jnp.where((shr(edges[b], 4 * c0) & 1) > 0, 1 << b, 0)

    mine = rsub == r0
    view_ref[0] = jnp.where(mine, bits, 0)
    view_ref[1] = jnp.where(mine & (into != 0), shr(out, 2 * c0) & 3, 0)
    view_ref[2] = into
    view_ref[3] = which
    view_ref[4] = k
    view_ref[5] = diag

    from_left = jnp.where(mine & ((slot >> 1) == c0), sent_left, 0)
    from_rows = [jnp.where(rk == r0, edge_ref[2 * c0 + v], 0) for v in range(2)]
    masks = [from_left] + from_rows
    place = sub * LANES + lane
    busy = jnp.where((masks[0] | masks[1] | masks[2]) != 0, place, NONE)
    state_ref[3] = busy
    for d in range(32):
        count_ref[d] = 0
    local = k - 240 * r0

    def pick(x, hit):
        return jnp.sum(jnp.where(hit, x, 0))

    def send_from(carried):
        spot, fetched, total = carried
        hit = place == spot
        left_over = jnp.where(hit, NONE, state_ref[3])
        state_ref[3] = left_over
        following = jnp.min(left_over)
        r = lax.shift_right_logical(spot, 8)
        picked_which = pick(which, hit)
        picked_row = pick(local, hit)
        picked = [pick(mask, hit) for mask in masks]
        slab_row = (lax.shift_right_logical(spot, 7) & 1) * 8 + (lax.shift_right_logical(spot, 4) & 7)
        sources = [
            2 * slab_row + (spot & 1),
            2 * picked_row + (lax.shift_right_logical(picked_which, 2 * c0) & 1),
            2 * picked_row + (lax.shift_right_logical(picked_which, 2 * c0 + 1) & 1),
        ]
        for source, nibbles in zip(sources, picked):

            def to_groups(carried):
                fetched, total = carried
                pltpu.make_async_copy(tiles_ref.at[source >> 1], fetched_ref.at[fetched], sem).start()
                begin_ref[fetched] = total
                for side in range(2):

                    def to_side(total, side=side):
                        for g in range(4 * side, 4 * side + 4):
                            on = lax.shift_right_logical(nibbles, 4 * g) & 1
                            d = r * 8 + g
                            seen = count_ref[d]
                            list_ref[2 * total] = seen * 32 + d
                            list_ref[2 * total + 1] = source
                            count_ref[d] = seen + on
                            total = total + on
                        return total

                    part = lax.shift_right_logical(nibbles, 16 * side) & 0xFFFF
                    total = lax.cond(part != 0, to_side, lambda t: t, total)
                return fetched + 1, total

            fetched, total = lax.cond(nibbles != 0, to_groups, lambda t: t, (fetched, total))
        return following, fetched, total

    first_spot = jnp.min(busy)
    _, fetched, total = lax.while_loop(
        lambda s: (s[0] < NONE) & (s[2] < 31 * CAPS[-1]), send_from, (first_spot, jnp.int32(0), jnp.int32(0))
    )
    words = []
    for p in range(8):
        pair = sent[2 * p] + sent[2 * p + 1]
        for r in range(4):
            words.append(jnp.where(rk == r, pair, 0))
    span = LANES // 2
    while len(words) > 1:
        if len(words) == 8:
            words = [capped(x) for x in words]
        merged = []
        first = (lane & span) == 0
        for x, y in zip(words[0::2], words[1::2]):
            z = jnp.where(first, x, y) + lanes_of(jnp.where(first, y, x), lane ^ span)
            merged.append(z if len(words) > 8 else capped(z))
        words = merged
        span //= 2
    word = words[0]
    while span >= 1:
        word = capped(word + lanes_of(word, lane ^ span))
        span //= 2
    by_slot = sent_left + lanes_of(sent_left, lane ^ 1)
    by_slot = by_slot + lanes_of(by_slot, lane ^ 64)
    by_slot = capped(by_slot + lanes_of(by_slot, lane ^ 32))
    by_slot = capped(by_slot + lanes_of(by_slot, lane ^ 16))
    group = (shr(lane, 4) & 1) | (shr(lane, 2) & 2) | (lane & 4)
    from_row = (shr(lane, 6) & 1) | (shr(lane, 4) & 2)
    word = capped(word + jnp.where(from_row == rsub, lanes_of(by_slot, 2 * group), 0))
    word = capped(word + pltpu.roll(word, 7, 0))
    most = jnp.zeros_like(word)
    for g in range(8):
        most = jnp.maximum(most, shr(word, 4 * g) & 15)
    most = jnp.where((sub & 1) == 0, most, 0)
    needed = jnp.max(most)
    chosen = jnp.int32(0)
    for cap in CAPS:
        chosen = chosen + (needed > cap).astype(jnp.int32)
    need_ref[0] = chosen
    begin_ref[fetched] = total

    @pl.loop(0, fetched)
    def _(n):
        pltpu.make_async_copy(tiles_ref.at[0], fetched_ref.at[n], sem).wait()

    @pl.loop(0, fetched)
    def _(n):
        chunk_ref[n] = packed_tile(fetched_ref[n], list_ref[2 * begin_ref[n] + 1] & 1)

    for index, send_ref in enumerate(send_refs):

        @pl.when((chosen == index) & (total > 0))
        def _(send_ref=send_ref):
            @pl.loop(0, fetched)
            def _(n):
                @pl.loop(begin_ref[n], begin_ref[n + 1])
                def _(t):
                    to = list_ref[2 * t]
                    pltpu.make_async_copy(chunk_ref.at[n], send_ref.at[to & 31, to >> 5], out_sem).start()

            @pl.loop(0, total)
            def _(t):
                pltpu.make_async_copy(chunk_ref.at[0], send_ref.at[0, 0], out_sem).wait()


def route_kernel(
    cap,
    view_ref,
    tiles_ref,
    program_ref,
    own_ref,
    slab_ref,
    base_ref,
    keep_ref,
    place_ref,
    state_ref,
    count_ref,
    kept_ref,
    fetched_ref,
    sem,
    slab_sem,
):
    slab_load = pltpu.make_async_copy(tiles_ref.at[:SLAB_ROWS], slab_ref, slab_sem)
    slab_load.start()
    r0 = lax.axis_index("row")
    c0 = lax.axis_index("col")
    me = r0 * 8 + c0
    lane = lax.broadcasted_iota(jnp.int32, (8, LANES), 1)
    sub = lax.broadcasted_iota(jnp.int32, (8, LANES), 0)
    place = sub * LANES + lane
    bits = view_ref[0]
    heads = view_ref[1]
    into = view_ref[2]
    which = view_ref[3]
    k = view_ref[4]
    diag = view_ref[5]
    for d in range(32):
        count_ref[d] = 0
    kept_ref[0] = 0

    def pick(x, hit):
        return jnp.sum(jnp.where(hit, x, 0))

    state_ref[0] = jnp.where(bits != 0, place, NONE)

    def arrive(spot):
        hit = place == spot
        left_over = jnp.where(hit, NONE, state_ref[0])
        state_ref[0] = left_over
        following = jnp.min(left_over)
        at = spot - 256 * r0
        picked = pick(bits, hit)
        picked_k = pick(k, hit)
        picked_which = pick(which, hit)
        source_row = picked_k // 240

        def put(entry, source, held_at):
            @pl.when(source == me)
            def _():
                kept = kept_ref[0]
                place_ref[entry] = jnp.where(kept < OWN, OWN_AT + kept, LOCAL + held_at)

                @pl.when(kept < OWN)
                def _():
                    pltpu.make_async_copy(tiles_ref.at[held_at >> 1], fetched_ref.at[kept], sem).start()
                    kept_ref[0] = kept + 1
                    kept_ref[1 + kept] = held_at

            @pl.when(source != me)
            def _():
                place_ref[entry] = source * cap + count_ref[source]
                count_ref[source] = count_ref[source] + 1

        @pl.when((picked >> 16) > 0)
        def _():
            put(4096 + at, r0 * 8 + ((at & 15) >> 1), 2 * (at >> 4) + (at & 1))

        @pl.loop(0, 16)
        def _(b):
            @pl.when(((picked >> b) & 1) > 0)
            def _():
                put(
                    at * 16 + b,
                    source_row * 8 + (b >> 1),
                    2 * (picked_k - 240 * source_row) + ((picked_which >> b) & 1),
                )

        return following

    lax.while_loop(lambda s: s < NONE, arrive, jnp.min(state_ref[0]))
    state_ref[1] = jnp.where(heads != 0, place, NONE)

    def follow(carried):
        spot, head_count, p = carried
        hit = place == spot
        left_over = jnp.where(hit, NONE, state_ref[1])
        state_ref[1] = left_over
        following = jnp.min(left_over)
        at = spot - 256 * r0
        i = at >> 4
        b = at & 15
        tails = pick(into, hit)
        ends = pick(heads, hit)
        self_slot = pick(diag, hit)
        most = jnp.int32(-1)
        for v in range(2):
            c = 2 * c0 + v
            entry = jnp.where(b == self_slot, 4096 + i * 16 + c, at * 16 + c)
            found = jnp.where(((ends >> v) & 1) > 0, place_ref[entry], -1)
            program_ref[p + 2 + v] = found
            most = jnp.maximum(most, found)

        def tail(a, carried):
            def add(carried):
                count, most = carried
                q = p + 4 + 2 * count
                x = place_ref[4096 + i * 16 + a]
                y = place_ref[jnp.where(a == self_slot, 4096 + i * 16 + b, (i * 16 + a) * 16 + b)]
                program_ref[q] = x
                program_ref[q + 1] = y
                return count + 1, jnp.maximum(most, jnp.maximum(x, y))

            return lax.cond(((tails >> a) & 1) > 0, add, lambda t: t, carried)

        count, most = lax.fori_loop(0, 16, tail, (jnp.int32(0), most))
        program_ref[p] = i + 16 * (most >= LOCAL).astype(jnp.int32)
        program_ref[p + 1] = count
        return following, head_count + 1, p + 4 + 2 * count

    _, head_count, end = lax.while_loop(
        lambda s: s[0] < NONE, follow, (jnp.min(state_ref[1]), jnp.int32(0), jnp.int32(2))
    )
    program_ref[0] = head_count
    program_ref[1] = end
    own_slot = 16 * sub + 2 * c0 + (lane >= 64).astype(jnp.int32)
    for half in range(2):
        held = jnp.broadcast_to(view_ref[4, pl.ds(2 * r0 + half, 1), :], (8, LANES))
        keep_ref[8 * half : 8 * half + 8, :] = (lanes_of(held, own_slot) >= 0).astype(jnp.int32)
    slab_load.wait()
    for i in range(SLAB_ROWS):
        keep = jnp.broadcast_to(keep_ref[i : i + 1, :], (64, LANES)) > 0
        base_ref[i] = jnp.where(keep, 1.5 * slab_ref[i].astype(jnp.float32), 0.0).astype(jnp.bfloat16)
    kept = kept_ref[0]

    @pl.loop(0, kept)
    def _(n):
        pltpu.make_async_copy(tiles_ref.at[0], fetched_ref.at[n], sem).wait()

    @pl.loop(0, kept)
    def _(n):
        own_ref[n] = packed_tile(fetched_ref[n], kept_ref[1 + n] & 1)


def apply_kernel(
    cap,
    program_hbm,
    got_ref,
    own_ref,
    tiles_ref,
    slab_ref,
    base_ref,
    keep_ref,
    out_ref,
    program_ref,
    cube_ref,
    touched_ref,
    patch_ref,
    spare_ref,
    sem,
    patch_sem,
    spare_sem,
    program_sem,
):
    load = pltpu.make_async_copy(program_hbm.at[:PREFIX], program_ref.at[:PREFIX], program_sem)
    load.start()
    write = pltpu.make_async_copy(base_ref, out_ref, sem)
    write.start()
    for i in range(SLAB_ROWS):
        touched_ref[i] = 0
    low = lax.broadcasted_iota(jnp.int32, (32, LANES), 1) < 64
    cube_ref[...] = jnp.zeros(cube_ref.shape, jnp.float32)
    load.wait()

    @pl.when(program_ref[1] > PREFIX)
    def _():
        rest = pltpu.make_async_copy(program_hbm, program_ref, program_sem)
        rest.start()
        rest.wait()

    def near(where):
        got_at = jnp.minimum(where, 32 * cap - 1)
        own_at = jnp.clip(where - OWN_AT, 0, OWN - 1)
        return jnp.where(where < OWN_AT, got_ref[got_at // cap, got_at % cap], own_ref[own_at])

    def anywhere(where):
        def far():
            copy = pltpu.make_async_copy(tiles_ref.at[(where - LOCAL) >> 1], spare_ref, spare_sem)
            copy.start()
            copy.wait()
            return packed_tile(spare_ref[...], where & 1)

        return lax.cond(where < LOCAL, lambda: near(where), far)

    def twice(tile):
        x = tile.astype(jnp.float32)
        y = pltpu.roll(x, 64, 1)
        zero = jnp.zeros_like(x)
        return jnp.concatenate(
            [jnp.where(low, x, zero), jnp.where(low, y, zero), jnp.where(low, zero, y), jnp.where(low, zero, x)], 0
        ).astype(jnp.bfloat16)

    def product(x, y):
        return jnp.dot(x, y, preferred_element_type=jnp.float32)

    def head(_, carried):
        p, touched = carried
        word = program_ref[p]
        count = program_ref[p + 1]
        i = word & 15
        ends = [program_ref[p + 2], program_ref[p + 3]]
        fresh = 1 - touched_ref[i]
        touched_ref[i] = 1
        touched_ref[16 + touched] = i

        def chain(tile_at):
            main = jnp.where(ends[0] >= 0, ends[0], ends[1])
            last = twice(tile_at(main))
            total = product(tile_at(program_ref[p + 4]), twice(tile_at(program_ref[p + 5])))

            def tail(t, total):
                q = p + 4 + 2 * t
                return total + product(tile_at(program_ref[q]), twice(tile_at(program_ref[q + 1])))

            squared = lax.fori_loop(1, count, tail, total).astype(jnp.bfloat16)
            cube_ref[i, (ends[0] < 0).astype(jnp.int32)] += product(squared, last)

            @pl.when((ends[0] >= 0) & (ends[1] >= 0))
            def _():
                cube_ref[i, 1] += product(squared, twice(tile_at(ends[1])))

        @pl.when(word < 16)
        def _():
            chain(near)

        @pl.when(word >= 16)
        def _():
            chain(anywhere)

        return p + 4 + 2 * count, touched + fresh

    _, touched = lax.fori_loop(0, program_ref[0], head, (jnp.int32(2), jnp.int32(0)))
    write.wait()

    def patch(i):
        return pltpu.make_async_copy(patch_ref.at[i], out_ref.at[i], patch_sem.at[i])

    @pl.loop(0, touched)
    def _(n):
        i = touched_ref[16 + n]
        x = cube_ref[i, 0]
        y = cube_ref[i, 1]
        cubed = jnp.concatenate(
            [jnp.where(low, x, pltpu.roll(y, 64, 1)), jnp.where(low, pltpu.roll(x, 64, 1), y)], 0
        )
        keep = jnp.broadcast_to(keep_ref[pl.ds(i, 1), :], (64, LANES)) > 0
        current = slab_ref[i].astype(jnp.float32)
        patch_ref[i] = jnp.where(keep, 1.5 * current - 0.5 * cubed, 0.0).astype(jnp.bfloat16)
        patch(i).start()

    @pl.loop(0, touched)
    def _(n):
        patch(touched_ref[16 + n]).wait()


def sparse_body(block_tiles, block_cols, block_counts):
    row_total = lax.axis_size("row")
    col_total = lax.axis_size("col")
    devices = row_total * col_total
    per_device = block_cols.shape[0]
    shown = pl.pallas_call(
        show_kernel,
        name="show",
        in_specs=[pl.BlockSpec(memory_space=pl.ANY)] * 2,
        out_shape=jax.ShapeDtypeStruct((devices, 1, per_device), jnp.int32),
        scratch_shapes=[
            pltpu.VMEM((2, per_device), jnp.int32),
            pltpu.VMEM((1, per_device), jnp.int32),
            pltpu.SemaphoreType.DMA,
            pltpu.SemaphoreType.DMA,
        ],
        compiler_params=pltpu.CompilerParams(vmem_limit_bytes=VMEM_LIMIT),
    )(
        pltpu.with_memory_space_constraint(block_cols.T, pltpu.HBM),
        pltpu.with_memory_space_constraint(block_counts.T, pltpu.HBM),
    )
    meta = lax.all_to_all(shown, ("row", "col"), 0, 0, tiled=True)
    vmem = pl.BlockSpec(memory_space=pltpu.VMEM)
    smem = pl.BlockSpec(memory_space=pltpu.SMEM)
    anywhere = pl.BlockSpec(memory_space=pl.ANY)
    limit = pltpu.CompilerParams(vmem_limit_bytes=VMEM_LIMIT)
    branch, view, *sends = pl.pallas_call(
        functools.partial(plan_kernel, SLAB_ROWS, NBLK // col_total),
        name="plan",
        in_specs=[vmem, anywhere],
        out_specs=(smem, vmem) + (anywhere,) * len(CAPS),
        out_shape=(pltpu.SMEM((1,), jnp.int32), jax.ShapeDtypeStruct((6, 8, LANES), jnp.int32))
        + tuple(pltpu.HBM((devices, cap, 32, LANES), jnp.bfloat16) for cap in CAPS),
        scratch_shapes=[
            pltpu.VMEM((8, 8, LANES), jnp.int32),
            pltpu.VMEM((16, 8, LANES), jnp.int32),
            pltpu.VMEM((4, 8, LANES), jnp.int32),
            pltpu.SMEM((512,), jnp.int32),
            pltpu.SMEM((32,), jnp.int32),
            pltpu.SMEM((256,), jnp.int32),
            pltpu.VMEM((248, 64, LANES), jnp.bfloat16),
            pltpu.VMEM((248, 32, LANES), jnp.bfloat16),
            pltpu.SemaphoreType.DMA,
            pltpu.SemaphoreType.DMA,
        ],
        compiler_params=limit,
    )(meta, block_tiles)

    def applied(cap, packed):
        got = lax.all_to_all(packed, ("row", "col"), 0, 0, tiled=True)
        program, own, slab, base, keep = pl.pallas_call(
            functools.partial(route_kernel, cap),
            name="route",
            in_specs=[vmem, anywhere],
            out_specs=(smem, vmem, vmem, vmem, vmem),
            out_shape=(
                jax.ShapeDtypeStruct((PROGRAM,), jnp.int32),
                jax.ShapeDtypeStruct((OWN, 32, LANES), jnp.bfloat16),
                jax.ShapeDtypeStruct((SLAB_ROWS, 64, LANES), jnp.bfloat16),
                jax.ShapeDtypeStruct((SLAB_ROWS, 64, LANES), jnp.bfloat16),
                jax.ShapeDtypeStruct((16, LANES), jnp.int32),
            ),
            scratch_shapes=[
                pltpu.SMEM((4096 + 256,), jnp.int32),
                pltpu.VMEM((2, 8, LANES), jnp.int32),
                pltpu.SMEM((32,), jnp.int32),
                pltpu.SMEM((1 + OWN,), jnp.int32),
                pltpu.VMEM((OWN, 64, LANES), jnp.bfloat16),
                pltpu.SemaphoreType.DMA,
                pltpu.SemaphoreType.DMA,
            ],
            compiler_params=limit,
            cost_estimate=pl.CostEstimate(flops=200000, bytes_accessed=400000, transcendentals=0),
        )(view, block_tiles)
        return pl.pallas_call(
            functools.partial(apply_kernel, cap),
            name="apply",
            in_specs=[anywhere, vmem, vmem, anywhere, vmem, vmem, vmem],
            out_specs=anywhere,
            out_shape=pltpu.HBM((SLAB_ROWS, 64, LANES), jnp.bfloat16),
            scratch_shapes=[
                pltpu.SMEM((PROGRAM,), jnp.int32),
                pltpu.VMEM((SLAB_ROWS, 2, 32, LANES), jnp.float32),
                pltpu.SMEM((32,), jnp.int32),
                pltpu.VMEM((SLAB_ROWS, 64, LANES), jnp.bfloat16),
                pltpu.VMEM((64, LANES), jnp.bfloat16),
                pltpu.SemaphoreType.DMA,
                pltpu.SemaphoreType.DMA((SLAB_ROWS,)),
                pltpu.SemaphoreType.DMA,
                pltpu.SemaphoreType.DMA,
            ],
            compiler_params=limit,
        )(program, got, own, block_tiles, slab, base, keep)

    branches = [functools.partial(applied, cap, packed) for cap, packed in zip(CAPS, sends)]

    def dense():
        own_group = meta.reshape(row_total, col_total, per_device)[:, lax.axis_index("col")].reshape(NBLK)
        pair = jnp.stack([own_group & 0xFFFF, own_group >> 16], axis=1)
        counts = jnp.sum((pair > 0).astype(jnp.int32), axis=1)
        start = lax.axis_index("row") * per_device
        own = lax.dynamic_slice_in_dim(pair, start, SLAB_ROWS, 0) - 1
        own_counts = lax.dynamic_slice_in_dim(counts, start, SLAB_ROWS, 0)[:, None]
        return dense_product(block_tiles, pair - 1, counts, own, own_counts)

    return lax.switch(branch[0], branches + [dense])


def solution(mesh):
    small = dict(mesh.shape) == {"row": 4, "col": 8}
    return jax.shard_map(
        sparse_body if small else dense_body,
        mesh=mesh,
        in_specs=(P("row", "col", None), P("row", "col"), P("row", "col")),
        out_specs=P("row", "col", None),
        check_vma=False,
    )
```

```python
import functools

import jax
import jax.numpy as jnp
from jax import lax
from jax.experimental import pallas as pl
from jax.experimental.pallas import tpu as pltpu
from jax.sharding import PartitionSpec as P

NBLK = 960
SLAB_ROWS = 12
LANES = 128
NONE = 1 << 30
LOCAL = 1 << 20
CAPS = (1, 2, 3, 4, 6)
OWN = 16
OWN_AT = 1 << 16
PREFIX = 1024
PROGRAM = 7168
VMEM_LIMIT = 24 << 20


def for_sending(x):
    return jax.tree.map(lambda a: a.astype(jnp.bfloat16) if a.dtype == jnp.float32 else a, x)


def passed_along(x, axis, by):
    length = lax.axis_size(axis)
    return lax.ppermute(x, axis, [(i, (i + by) % length) for i in range(length)])


def tile_products(running, visitor, first_group, panel, own_cols, own_valid, width):
    left_tiles, left_cols, left_counts = visitor
    panel_tiles, panel_cols, panel_counts = panel
    row_count = left_cols.shape[0]
    group_count = left_cols.shape[1]
    slot_count = left_cols.shape[2]
    block_size = left_tiles.shape[2]
    offset = first_group * width
    group_tiles = lax.dynamic_slice_in_dim(panel_tiles, offset, group_count * width, 0)
    group_tiles = group_tiles.reshape(group_count, width, block_size, slot_count, block_size)
    group_cols = lax.dynamic_slice_in_dim(panel_cols, offset, group_count * width, 0).reshape(
        group_count, width, slot_count
    )
    group_counts = lax.dynamic_slice_in_dim(panel_counts, offset, group_count * width, 0).reshape(
        group_count, width
    )
    group_valid = jnp.arange(slot_count, dtype=jnp.int32)[None, None, :] < group_counts[:, :, None]
    left_valid = jnp.arange(slot_count, dtype=jnp.int32)[None, None, :] < left_counts[:, :, None]
    onehot = left_cols[:, :, :, None] == jnp.arange(width, dtype=jnp.int32)[None, None, None, :]
    matched = group_cols[None, :, None, :, :, None] == own_cols[:, None, None, None, None, :]
    matched = (
        matched & group_valid[None, :, None, :, :, None] & own_valid[:, None, None, None, None, :]
    )
    matched = matched & onehot[:, :, :, :, None, None] & left_valid[:, :, :, None, None, None]
    chosen = jnp.einsum(
        "igukwv,gkywz->iguyvz",
        matched.astype(jnp.bfloat16),
        group_tiles,
        preferred_element_type=jnp.float32,
    ).astype(jnp.bfloat16)
    left_blocks = left_tiles.reshape(row_count, group_count, block_size, slot_count, block_size)
    return running + jnp.einsum(
        "igxuy,iguyvz->ixvz", left_blocks, chosen, preferred_element_type=jnp.float32
    )


def restricted_product(left_parts, panel, own_cols, own_valid):
    col_total = lax.axis_size("col")
    row_total = lax.axis_size("row")
    width = NBLK // col_total
    slab_count = own_cols.shape[0]
    slot_count = own_cols.shape[1]
    block_size = panel[0].shape[1]
    initial = jnp.zeros((slab_count, block_size, slot_count, block_size), jnp.float32)
    ratio = col_total // row_total
    row_index = lax.axis_index("row")
    col_index = lax.axis_index("col")
    moving = left_parts
    for bit_number in range(row_total.bit_length() - 1):
        arrived = jax.tree.map(
            lambda part, own: part.astype(own.dtype),
            passed_along(for_sending(moving), "col", -(ratio << bit_number)),
            moving,
        )
        flagged = row_index // (1 << bit_number) % 2 == 1

        def select_one(incoming, current):
            return jnp.where(flagged, incoming, current)

        moving = jax.tree.map(select_one, arrived, moving)
    anchor = col_index + ratio * row_index

    def advance(section_index, carried):
        running, visiting = carried
        running = tile_products(
            running,
            visiting,
            (anchor + section_index) % col_total,
            panel,
            own_cols,
            own_valid,
            width,
        )
        visiting = jax.tree.map(
            lambda part, own: part.astype(own.dtype),
            passed_along(for_sending(visiting), "col", -1),
            visiting,
        )
        return (running, visiting)

    running, moving = lax.fori_loop(0, col_total - 1, advance, (initial, moving))
    return tile_products(
        running, moving, (anchor + col_total - 1) % col_total, panel, own_cols, own_valid, width
    )


def over_rows(x):
    row_total = lax.axis_size("row")
    return lax.all_to_all(jnp.broadcast_to(x, (row_total,) + x.shape), "row", 0, 0, tiled=True)


def dense_body(block_tiles, block_cols, block_counts):
    panel_cols = over_rows(block_cols).reshape(NBLK, block_cols.shape[1])
    panel_counts = over_rows(block_counts).reshape(NBLK)
    return dense_product(
        block_tiles, panel_cols, panel_counts, block_cols[:SLAB_ROWS], block_counts[:SLAB_ROWS]
    )


def dense_product(block_tiles, panel_cols, panel_counts, own_cols, own_counts):
    block_size = block_tiles.shape[1]
    slot_count = own_cols.shape[1]
    panel_tiles = over_rows(block_tiles).reshape((NBLK,) + block_tiles.shape[1:])
    panel = (panel_tiles, panel_cols, panel_counts)
    slab_tiles = block_tiles[:SLAB_ROWS]
    own_valid = jnp.arange(slot_count, dtype=jnp.int32)[None, :] < own_counts
    first_parts = (
        slab_tiles.reshape(SLAB_ROWS, 1, block_size, slot_count * block_size),
        own_cols.reshape(SLAB_ROWS, 1, slot_count),
        own_counts,
    )
    squared = restricted_product(first_parts, panel, own_cols, own_valid)
    squared = squared.reshape(SLAB_ROWS, 1, block_size, slot_count * block_size).astype(
        jnp.bfloat16
    )
    second_parts = (squared, own_cols.reshape(SLAB_ROWS, 1, slot_count), own_counts)
    cubed = restricted_product(second_parts, panel, own_cols, own_valid)
    current = slab_tiles.reshape(SLAB_ROWS, block_size, slot_count, block_size).astype(jnp.float32)
    result = jnp.where(own_valid[:, None, :, None], 1.5 * current - 0.5 * cubed, jnp.float32(0.0))
    return result.reshape(SLAB_ROWS, block_size, slot_count * block_size).astype(jnp.bfloat16)


def lanes_of(x, index):
    return jnp.take_along_axis(x, index, axis=1)


def shr(x, n):
    return lax.shift_right_logical(x, jnp.broadcast_to(jnp.int32(n), x.shape) if jnp.ndim(n) == 0 else n)


def shl(x, n):
    return lax.shift_left(x, jnp.broadcast_to(jnp.int32(n), x.shape) if jnp.ndim(n) == 0 else n)


SEVENS = 0x77777777
EIGHTS = -(1 << 31) | 0x08888888


def capped(x):
    high = x & jnp.int32(EIGHTS)
    return (x & jnp.int32(SEVENS)) | (high - shr(high, 3))


def packed_tile(tile, high):
    tile = tile.astype(jnp.float32)
    tile = jnp.where(high > 0, pltpu.roll(tile, 64, 1), tile)
    upper = lax.broadcasted_iota(jnp.int32, (32, LANES), 1) >= 64
    return jnp.where(upper, pltpu.roll(tile[32:], 64, 1), tile[:32]).astype(jnp.bfloat16)


def show_kernel(cols_hbm, counts_hbm, out_ref, cols_ref, counts_ref, cols_sem, counts_sem):
    cols_load = pltpu.make_async_copy(cols_hbm, cols_ref, cols_sem)
    counts_load = pltpu.make_async_copy(counts_hbm, counts_ref, counts_sem)
    cols_load.start()
    counts_load.start()
    cols_load.wait()
    counts_load.wait()
    counts = counts_ref[...]
    first = jnp.where(counts > 0, cols_ref[0:1] + 1, 0)
    second = jnp.where(counts > 1, cols_ref[1:2] + 1, 0)
    out_ref[...] = jnp.broadcast_to(first | (second << 16), out_ref.shape)


def plan_kernel(rows, width, meta_ref, tiles_ref, need_ref, view_ref, *rest):
    send_refs = rest[: len(CAPS)]
    (
        part_ref, edge_ref, state_ref, list_ref, count_ref, begin_ref, fetched_ref, chunk_ref, sem, out_sem
    ) = rest[len(CAPS) :]
    r0 = lax.axis_index("row")
    c0 = lax.axis_index("col")
    lane = lax.broadcasted_iota(jnp.int32, (8, LANES), 1)
    sub = lax.broadcasted_iota(jnp.int32, (8, LANES), 0)
    slot = lane & 15
    base = lane - slot
    group = slot >> 1
    odd = slot & 1
    doubled = 2 * sub
    for r in range(4):
        for c in range(8):
            piece = meta_ref[8 * r + c]
            part_ref[2 * r, c : c + 1, :] = piece[:, :LANES]
            part_ref[2 * r + 1, c : c + 1, : piece.shape[1] - LANES] = piece[:, LANES:]
    parts = [part_ref[j] for j in range(8)]
    for r in range(4):
        for half in range(2):
            i8 = (lane >> 4) + 8 * half
            own = jnp.where(i8 < rows, lanes_of(parts[2 * r], i8), 0)
            col = jnp.sum(jnp.where(sub == group, own, 0), axis=0, keepdims=True)
            col = shr(col, 16 * odd[:1]) & 0xFFFF
            k = group[:1] * width + col - 1
            rk = (k >= 240).astype(jnp.int32) + (k >= 480).astype(jnp.int32) + (k >= 720).astype(jnp.int32)
            n = k - 240 * rk
            where_k = jnp.where(col > 0, 2 * rk + (n >> 7), -1)
            at = jnp.broadcast_to(n & (LANES - 1), (8, LANES))
            piece_k = jnp.broadcast_to(where_k, (8, LANES))
            found = jnp.zeros((8, LANES), jnp.int32)
            for j in range(8):
                found = jnp.where(piece_k == j, lanes_of(parts[j], at), found)
            b0 = own & 0xFFFF
            b1 = shr(own, 16)
            g0 = found & 0xFFFF
            g1 = shr(found, 16)
            at0 = (b0 > 0) & (g0 == b0)
            at0_high = (b0 > 0) & (g1 == b0)
            at1 = (b1 > 0) & (g0 == b1)
            at1_high = (b1 > 0) & (g1 == b1)
            high = jnp.where(at0_high, 1, 0) | jnp.where(at1_high, 2, 0)
            any_edge = jnp.where(at0, 1, 0) | jnp.where(at1, 2, 0) | high
            s = 2 * r + half
            state_ref[0, s : s + 1, :] = jnp.sum(shl(any_edge, doubled), axis=0, keepdims=True)
            state_ref[1, s : s + 1, :] = jnp.sum(shl(high, doubled), axis=0, keepdims=True)
            state_ref[2, s : s + 1, :] = jnp.where(col > 0, k, -1)
    out = state_ref[0]
    which = state_ref[1]
    k = state_ref[2]
    rk = (k >= 240).astype(jnp.int32) + (k >= 480).astype(jnp.int32) + (k >= 720).astype(jnp.int32)
    rsub = sub >> 1
    row = (sub & 1) * 8 + (lane >> 4)

    into = jnp.zeros_like(out)
    for a in range(16):
        into = into | shl(shr(lanes_of(out, base + a), slot) & 1, a)
    spread = (out | shr(out, 1)) & 0x5555
    spread = (spread | shl(spread, 8)) & 0x00FF00FF
    spread = (spread | shl(spread, 4)) & 0x0F0F0F0F
    spread = (spread | shl(spread, 2)) & 0x11111111
    itself = rsub * 240 + row
    on_diag = (k == itself) & (k >= 0)
    first_slot = 2 * (rsub * (240 // width))
    diag = jnp.full_like(slot, -1)
    for v in range(2):
        held = lanes_of(k, base + first_slot + v)
        diag = jnp.where((held == itself) & (held >= 0), first_slot + v, diag)
    has_diag = diag >= 0
    diag_at = base + jnp.maximum(diag, 0)
    left = jnp.zeros_like(out)
    extra = jnp.zeros_like(out)
    edges = []
    for b in range(16):
        has = (shr(out, b) & 1) > 0
        heads = lanes_of(spread, base + b)
        left = left | jnp.where(has, heads, 0)
        edge = jnp.where(has, heads | jnp.where(into != 0, 1 << (4 * (b // 2)), 0), 0)
        extra = extra | jnp.where((slot == b) & has_diag, lanes_of(edge, diag_at), 0)
        edges.append(jnp.where(on_diag, 0, edge))
    left = left | extra

    fifteen = jnp.full_like(out, 15)
    sent_left = left & ~shl(fifteen, 4 * (slot >> 1))
    sent = []
    bits = jnp.where((shr(left, 4 * c0) & 1) > 0, 1 << 16, 0)
    for b in range(16):
        own_nibble = (15 << (4 * (b // 2))) if b < 14 else -(1 << 28)
        sent.append(edges[b] & ~jnp.where(rk == rsub, jnp.int32(own_nibble), 0))
        edge_ref[b] = sent[b]
        bits = bits | jnp.where((shr(edges[b], 4 * c0) & 1) > 0, 1 << b, 0)

    mine = rsub == r0
    view_ref[0] = jnp.where(mine, bits, 0)
    view_ref[1] = jnp.where(mine & (into != 0), shr(out, 2 * c0) & 3, 0)
    view_ref[2] = into
    view_ref[3] = which
    view_ref[4] = k
    view_ref[5] = diag

    from_left = jnp.where(mine & ((slot >> 1) == c0), sent_left, 0)
    from_rows = [jnp.where(rk == r0, edge_ref[2 * c0 + v], 0) for v in range(2)]
    masks = [from_left] + from_rows
    place = sub * LANES + lane
    busy = jnp.where((masks[0] | masks[1] | masks[2]) != 0, place, NONE)
    state_ref[3] = busy
    for d in range(32):
        count_ref[d] = 0
    local = k - 240 * r0

    def pick(x, hit):
        return jnp.sum(jnp.where(hit, x, 0))

    def send_from(carried):
        spot, fetched, total = carried
        hit = place == spot
        left_over = jnp.where(hit, NONE, state_ref[3])
        state_ref[3] = left_over
        following = jnp.min(left_over)
        r = lax.shift_right_logical(spot, 8)
        picked_which = pick(which, hit)
        picked_row = pick(local, hit)
        picked = [pick(mask, hit) for mask in masks]
        slab_row = (lax.shift_right_logical(spot, 7) & 1) * 8 + (lax.shift_right_logical(spot, 4) & 7)
        sources = [
            2 * slab_row + (spot & 1),
            2 * picked_row + (lax.shift_right_logical(picked_which, 2 * c0) & 1),
            2 * picked_row + (lax.shift_right_logical(picked_which, 2 * c0 + 1) & 1),
        ]
        for source, nibbles in zip(sources, picked):

            def to_groups(carried):
                fetched, total = carried
                pltpu.make_async_copy(tiles_ref.at[source >> 1], fetched_ref.at[fetched], sem).start()
                begin_ref[fetched] = total
                for side in range(2):

                    def to_side(total, side=side):
                        for g in range(4 * side, 4 * side + 4):
                            on = lax.shift_right_logical(nibbles, 4 * g) & 1
                            d = r * 8 + g
                            seen = count_ref[d]
                            list_ref[2 * total] = seen * 32 + d
                            list_ref[2 * total + 1] = source
                            count_ref[d] = seen + on
                            total = total + on
                        return total

                    part = lax.shift_right_logical(nibbles, 16 * side) & 0xFFFF
                    total = lax.cond(part != 0, to_side, lambda t: t, total)
                return fetched + 1, total

            fetched, total = lax.cond(nibbles != 0, to_groups, lambda t: t, (fetched, total))
        return following, fetched, total

    first_spot = jnp.min(busy)
    _, fetched, total = lax.while_loop(
        lambda s: (s[0] < NONE) & (s[2] < 31 * CAPS[-1]), send_from, (first_spot, jnp.int32(0), jnp.int32(0))
    )
    words = []
    for p in range(8):
        pair = sent[2 * p] + sent[2 * p + 1]
        for r in range(4):
            words.append(jnp.where(rk == r, pair, 0))
    span = LANES // 2
    while len(words) > 1:
        if len(words) == 8:
            words = [capped(x) for x in words]
        merged = []
        first = (lane & span) == 0
        for x, y in zip(words[0::2], words[1::2]):
            z = jnp.where(first, x, y) + lanes_of(jnp.where(first, y, x), lane ^ span)
            merged.append(z if len(words) > 8 else capped(z))
        words = merged
        span //= 2
    word = words[0]
    while span >= 1:
        word = capped(word + lanes_of(word, lane ^ span))
        span //= 2
    by_slot = sent_left + lanes_of(sent_left, lane ^ 1)
    by_slot = by_slot + lanes_of(by_slot, lane ^ 64)
    by_slot = capped(by_slot + lanes_of(by_slot, lane ^ 32))
    by_slot = capped(by_slot + lanes_of(by_slot, lane ^ 16))
    group = (shr(lane, 4) & 1) | (shr(lane, 2) & 2) | (lane & 4)
    from_row = (shr(lane, 6) & 1) | (shr(lane, 4) & 2)
    word = capped(word + jnp.where(from_row == rsub, lanes_of(by_slot, 2 * group), 0))
    word = capped(word + pltpu.roll(word, 7, 0))
    most = jnp.zeros_like(word)
    for g in range(8):
        most = jnp.maximum(most, shr(word, 4 * g) & 15)
    most = jnp.where((sub & 1) == 0, most, 0)
    needed = jnp.max(most)
    chosen = jnp.int32(0)
    for cap in CAPS:
        chosen = chosen + (needed > cap).astype(jnp.int32)
    need_ref[0] = chosen
    begin_ref[fetched] = total

    @pl.loop(0, fetched)
    def _(n):
        pltpu.make_async_copy(tiles_ref.at[0], fetched_ref.at[n], sem).wait()

    for index, send_ref in enumerate(send_refs):

        @pl.when((chosen == index) & (total > 0))
        def _(send_ref=send_ref):
            @pl.loop(0, fetched)
            def _(n):
                chunk_ref[n] = packed_tile(fetched_ref[n], list_ref[2 * begin_ref[n] + 1] & 1)

                @pl.loop(begin_ref[n], begin_ref[n + 1])
                def _(t):
                    to = list_ref[2 * t]
                    pltpu.make_async_copy(chunk_ref.at[n], send_ref.at[to & 31, to >> 5], out_sem).start()

            @pl.loop(0, total)
            def _(t):
                pltpu.make_async_copy(chunk_ref.at[0], send_ref.at[0, 0], out_sem).wait()


def route_kernel(
    cap,
    view_ref,
    tiles_ref,
    program_ref,
    own_ref,
    slab_ref,
    base_ref,
    keep_ref,
    place_ref,
    state_ref,
    count_ref,
    kept_ref,
    fetched_ref,
    sem,
    slab_sem,
):
    slab_load = pltpu.make_async_copy(tiles_ref.at[:SLAB_ROWS], slab_ref, slab_sem)
    slab_load.start()
    r0 = lax.axis_index("row")
    c0 = lax.axis_index("col")
    me = r0 * 8 + c0
    lane = lax.broadcasted_iota(jnp.int32, (8, LANES), 1)
    sub = lax.broadcasted_iota(jnp.int32, (8, LANES), 0)
    place = sub * LANES + lane
    bits = view_ref[0]
    heads = view_ref[1]
    into = view_ref[2]
    which = view_ref[3]
    k = view_ref[4]
    diag = view_ref[5]
    for d in range(32):
        count_ref[d] = 0
    kept_ref[0] = 0

    def pick(x, hit):
        return jnp.sum(jnp.where(hit, x, 0))

    state_ref[0] = jnp.where(bits != 0, place, NONE)

    def arrive(spot):
        hit = place == spot
        left_over = jnp.where(hit, NONE, state_ref[0])
        state_ref[0] = left_over
        following = jnp.min(left_over)
        at = spot - 256 * r0
        picked = pick(bits, hit)
        picked_k = pick(k, hit)
        picked_which = pick(which, hit)
        source_row = picked_k // 240

        def put(entry, source, held_at):
            @pl.when(source == me)
            def _():
                kept = kept_ref[0]
                place_ref[entry] = jnp.where(kept < OWN, OWN_AT + kept, LOCAL + held_at)

                @pl.when(kept < OWN)
                def _():
                    pltpu.make_async_copy(tiles_ref.at[held_at >> 1], fetched_ref.at[kept], sem).start()
                    kept_ref[0] = kept + 1
                    kept_ref[1 + kept] = held_at

            @pl.when(source != me)
            def _():
                place_ref[entry] = source * cap + count_ref[source]
                count_ref[source] = count_ref[source] + 1

        @pl.when((picked >> 16) > 0)
        def _():
            put(4096 + at, r0 * 8 + ((at & 15) >> 1), 2 * (at >> 4) + (at & 1))

        @pl.loop(0, 16)
        def _(b):
            @pl.when(((picked >> b) & 1) > 0)
            def _():
                put(
                    at * 16 + b,
                    source_row * 8 + (b >> 1),
                    2 * (picked_k - 240 * source_row) + ((picked_which >> b) & 1),
                )

        return following

    lax.while_loop(lambda s: s < NONE, arrive, jnp.min(state_ref[0]))
    state_ref[1] = jnp.where(heads != 0, place, NONE)

    def follow(carried):
        spot, head_count, p = carried
        hit = place == spot
        left_over = jnp.where(hit, NONE, state_ref[1])
        state_ref[1] = left_over
        following = jnp.min(left_over)
        at = spot - 256 * r0
        i = at >> 4
        b = at & 15
        tails = pick(into, hit)
        ends = pick(heads, hit)
        self_slot = pick(diag, hit)
        most = jnp.int32(-1)
        for v in range(2):
            c = 2 * c0 + v
            entry = jnp.where(b == self_slot, 4096 + i * 16 + c, at * 16 + c)
            found = jnp.where(((ends >> v) & 1) > 0, place_ref[entry], -1)
            program_ref[p + 2 + v] = found
            most = jnp.maximum(most, found)

        def tail(a, carried):
            def add(carried):
                count, most = carried
                q = p + 4 + 2 * count
                x = place_ref[4096 + i * 16 + a]
                y = place_ref[jnp.where(a == self_slot, 4096 + i * 16 + b, (i * 16 + a) * 16 + b)]
                program_ref[q] = x
                program_ref[q + 1] = y
                return count + 1, jnp.maximum(most, jnp.maximum(x, y))

            return lax.cond(((tails >> a) & 1) > 0, add, lambda t: t, carried)

        count, most = lax.fori_loop(0, 16, tail, (jnp.int32(0), most))
        program_ref[p] = i + 16 * (most >= LOCAL).astype(jnp.int32)
        program_ref[p + 1] = count
        return following, head_count + 1, p + 4 + 2 * count

    _, head_count, end = lax.while_loop(
        lambda s: s[0] < NONE, follow, (jnp.min(state_ref[1]), jnp.int32(0), jnp.int32(2))
    )
    program_ref[0] = head_count
    program_ref[1] = end
    own_slot = 16 * sub + 2 * c0 + (lane >= 64).astype(jnp.int32)
    for half in range(2):
        held = jnp.broadcast_to(view_ref[4, pl.ds(2 * r0 + half, 1), :], (8, LANES))
        keep_ref[8 * half : 8 * half + 8, :] = (lanes_of(held, own_slot) >= 0).astype(jnp.int32)
    slab_load.wait()
    for i in range(SLAB_ROWS):
        keep = jnp.broadcast_to(keep_ref[i : i + 1, :], (64, LANES)) > 0
        base_ref[i] = jnp.where(keep, 1.5 * slab_ref[i].astype(jnp.float32), 0.0).astype(jnp.bfloat16)
    kept = kept_ref[0]

    @pl.loop(0, kept)
    def _(n):
        pltpu.make_async_copy(tiles_ref.at[0], fetched_ref.at[n], sem).wait()

    @pl.loop(0, kept)
    def _(n):
        own_ref[n] = packed_tile(fetched_ref[n], kept_ref[1 + n] & 1)


def apply_kernel(
    cap,
    program_hbm,
    got_ref,
    own_ref,
    tiles_ref,
    slab_ref,
    base_ref,
    keep_ref,
    out_ref,
    program_ref,
    cube_ref,
    touched_ref,
    patch_ref,
    spare_ref,
    sem,
    patch_sem,
    spare_sem,
    program_sem,
):
    load = pltpu.make_async_copy(program_hbm.at[:PREFIX], program_ref.at[:PREFIX], program_sem)
    load.start()
    write = pltpu.make_async_copy(base_ref, out_ref, sem)
    write.start()
    for i in range(SLAB_ROWS):
        touched_ref[i] = 0
    low = lax.broadcasted_iota(jnp.int32, (32, LANES), 1) < 64
    cube_ref[...] = jnp.zeros(cube_ref.shape, jnp.float32)
    load.wait()

    @pl.when(program_ref[1] > PREFIX)
    def _():
        rest = pltpu.make_async_copy(program_hbm, program_ref, program_sem)
        rest.start()
        rest.wait()

    def near(where):
        got_at = jnp.minimum(where, 32 * cap - 1)
        own_at = jnp.clip(where - OWN_AT, 0, OWN - 1)
        return jnp.where(where < OWN_AT, got_ref[got_at // cap, got_at % cap], own_ref[own_at])

    def anywhere(where):
        def far():
            copy = pltpu.make_async_copy(tiles_ref.at[(where - LOCAL) >> 1], spare_ref, spare_sem)
            copy.start()
            copy.wait()
            return packed_tile(spare_ref[...], where & 1)

        return lax.cond(where < LOCAL, lambda: near(where), far)

    def twice(tile):
        x = tile.astype(jnp.float32)
        y = pltpu.roll(x, 64, 1)
        zero = jnp.zeros_like(x)
        return jnp.concatenate(
            [jnp.where(low, x, zero), jnp.where(low, y, zero), jnp.where(low, zero, y), jnp.where(low, zero, x)], 0
        ).astype(jnp.bfloat16)

    def product(x, y):
        return jnp.dot(x, y, preferred_element_type=jnp.float32)

    def head(_, carried):
        p, touched = carried
        word = program_ref[p]
        count = program_ref[p + 1]
        i = word & 15
        ends = [program_ref[p + 2], program_ref[p + 3]]
        fresh = 1 - touched_ref[i]
        touched_ref[i] = 1
        touched_ref[16 + touched] = i

        def chain(tile_at):
            main = jnp.where(ends[0] >= 0, ends[0], ends[1])
            last = twice(tile_at(main))
            total = product(tile_at(program_ref[p + 4]), twice(tile_at(program_ref[p + 5])))

            def tail(t, total):
                q = p + 4 + 2 * t
                return total + product(tile_at(program_ref[q]), twice(tile_at(program_ref[q + 1])))

            squared = lax.fori_loop(1, count, tail, total).astype(jnp.bfloat16)
            cube_ref[i, (ends[0] < 0).astype(jnp.int32)] += product(squared, last)

            @pl.when((ends[0] >= 0) & (ends[1] >= 0))
            def _():
                cube_ref[i, 1] += product(squared, twice(tile_at(ends[1])))

        @pl.when(word < 16)
        def _():
            chain(near)

        @pl.when(word >= 16)
        def _():
            chain(anywhere)

        return p + 4 + 2 * count, touched + fresh

    _, touched = lax.fori_loop(0, program_ref[0], head, (jnp.int32(2), jnp.int32(0)))
    write.wait()

    def patch(i):
        return pltpu.make_async_copy(patch_ref.at[i], out_ref.at[i], patch_sem.at[i])

    @pl.loop(0, touched)
    def _(n):
        i = touched_ref[16 + n]
        x = cube_ref[i, 0]
        y = cube_ref[i, 1]
        cubed = jnp.concatenate(
            [jnp.where(low, x, pltpu.roll(y, 64, 1)), jnp.where(low, pltpu.roll(x, 64, 1), y)], 0
        )
        keep = jnp.broadcast_to(keep_ref[pl.ds(i, 1), :], (64, LANES)) > 0
        current = slab_ref[i].astype(jnp.float32)
        patch_ref[i] = jnp.where(keep, 1.5 * current - 0.5 * cubed, 0.0).astype(jnp.bfloat16)
        patch(i).start()

    @pl.loop(0, touched)
    def _(n):
        patch(touched_ref[16 + n]).wait()


def sparse_body(block_tiles, block_cols, block_counts):
    row_total = lax.axis_size("row")
    col_total = lax.axis_size("col")
    devices = row_total * col_total
    per_device = block_cols.shape[0]
    shown = pl.pallas_call(
        show_kernel,
        name="show",
        in_specs=[pl.BlockSpec(memory_space=pl.ANY)] * 2,
        out_shape=jax.ShapeDtypeStruct((devices, 1, per_device), jnp.int32),
        scratch_shapes=[
            pltpu.VMEM((2, per_device), jnp.int32),
            pltpu.VMEM((1, per_device), jnp.int32),
            pltpu.SemaphoreType.DMA,
            pltpu.SemaphoreType.DMA,
        ],
        compiler_params=pltpu.CompilerParams(vmem_limit_bytes=VMEM_LIMIT),
    )(
        pltpu.with_memory_space_constraint(block_cols.T, pltpu.HBM),
        pltpu.with_memory_space_constraint(block_counts.T, pltpu.HBM),
    )
    meta = lax.all_to_all(shown, ("row", "col"), 0, 0, tiled=True)
    vmem = pl.BlockSpec(memory_space=pltpu.VMEM)
    smem = pl.BlockSpec(memory_space=pltpu.SMEM)
    anywhere = pl.BlockSpec(memory_space=pl.ANY)
    limit = pltpu.CompilerParams(vmem_limit_bytes=VMEM_LIMIT)
    branch, view, *sends = pl.pallas_call(
        functools.partial(plan_kernel, SLAB_ROWS, NBLK // col_total),
        name="plan",
        in_specs=[vmem, anywhere],
        out_specs=(smem, vmem) + (anywhere,) * len(CAPS),
        out_shape=(pltpu.SMEM((1,), jnp.int32), jax.ShapeDtypeStruct((6, 8, LANES), jnp.int32))
        + tuple(pltpu.HBM((devices, cap, 32, LANES), jnp.bfloat16) for cap in CAPS),
        scratch_shapes=[
            pltpu.VMEM((8, 8, LANES), jnp.int32),
            pltpu.VMEM((16, 8, LANES), jnp.int32),
            pltpu.VMEM((4, 8, LANES), jnp.int32),
            pltpu.SMEM((512,), jnp.int32),
            pltpu.SMEM((32,), jnp.int32),
            pltpu.SMEM((256,), jnp.int32),
            pltpu.VMEM((248, 64, LANES), jnp.bfloat16),
            pltpu.VMEM((248, 32, LANES), jnp.bfloat16),
            pltpu.SemaphoreType.DMA,
            pltpu.SemaphoreType.DMA,
        ],
        compiler_params=limit,
    )(meta, block_tiles)

    def applied(cap, packed):
        got = lax.all_to_all(packed, ("row", "col"), 0, 0, tiled=True)
        program, own, slab, base, keep = pl.pallas_call(
            functools.partial(route_kernel, cap),
            name="route",
            in_specs=[vmem, anywhere],
            out_specs=(smem, vmem, vmem, vmem, vmem),
            out_shape=(
                jax.ShapeDtypeStruct((PROGRAM,), jnp.int32),
                jax.ShapeDtypeStruct((OWN, 32, LANES), jnp.bfloat16),
                jax.ShapeDtypeStruct((SLAB_ROWS, 64, LANES), jnp.bfloat16),
                jax.ShapeDtypeStruct((SLAB_ROWS, 64, LANES), jnp.bfloat16),
                jax.ShapeDtypeStruct((16, LANES), jnp.int32),
            ),
            scratch_shapes=[
                pltpu.SMEM((4096 + 256,), jnp.int32),
                pltpu.VMEM((2, 8, LANES), jnp.int32),
                pltpu.SMEM((32,), jnp.int32),
                pltpu.SMEM((1 + OWN,), jnp.int32),
                pltpu.VMEM((OWN, 64, LANES), jnp.bfloat16),
                pltpu.SemaphoreType.DMA,
                pltpu.SemaphoreType.DMA,
            ],
            compiler_params=limit,
            cost_estimate=pl.CostEstimate(flops=200000, bytes_accessed=400000, transcendentals=0),
        )(view, block_tiles)
        return pl.pallas_call(
            functools.partial(apply_kernel, cap),
            name="apply",
            in_specs=[anywhere, vmem, vmem, anywhere, vmem, vmem, vmem],
            out_specs=anywhere,
            out_shape=pltpu.HBM((SLAB_ROWS, 64, LANES), jnp.bfloat16),
            scratch_shapes=[
                pltpu.SMEM((PROGRAM,), jnp.int32),
                pltpu.VMEM((SLAB_ROWS, 2, 32, LANES), jnp.float32),
                pltpu.SMEM((32,), jnp.int32),
                pltpu.VMEM((SLAB_ROWS, 64, LANES), jnp.bfloat16),
                pltpu.VMEM((64, LANES), jnp.bfloat16),
                pltpu.SemaphoreType.DMA,
                pltpu.SemaphoreType.DMA((SLAB_ROWS,)),
                pltpu.SemaphoreType.DMA,
                pltpu.SemaphoreType.DMA,
            ],
            compiler_params=limit,
        )(program, got, own, block_tiles, slab, base, keep)

    branches = [functools.partial(applied, cap, packed) for cap, packed in zip(CAPS, sends)]

    def dense():
        own_group = meta.reshape(row_total, col_total, per_device)[:, lax.axis_index("col")].reshape(NBLK)
        pair = jnp.stack([own_group & 0xFFFF, own_group >> 16], axis=1)
        counts = jnp.sum((pair > 0).astype(jnp.int32), axis=1)
        start = lax.axis_index("row") * per_device
        own = lax.dynamic_slice_in_dim(pair, start, SLAB_ROWS, 0) - 1
        own_counts = lax.dynamic_slice_in_dim(counts, start, SLAB_ROWS, 0)[:, None]
        return dense_product(block_tiles, pair - 1, counts, own, own_counts)

    return lax.switch(branch[0], branches + [dense])


def solution(mesh):
    small = dict(mesh.shape) == {"row": 4, "col": 8}
    return jax.shard_map(
        sparse_body if small else dense_body,
        mesh=mesh,
        in_specs=(P("row", "col", None), P("row", "col"), P("row", "col")),
        out_specs=P("row", "col", None),
        check_vma=False,
    )
```
